256 devices in a mesh: narrow: 8 (over y, core), wide: 32 (over x, z).
Axes of the slice: x: 4, y: 4, z: 8, core: 2. Of those that a mesh axis runs over, the one named last changes fastest.
Arguments:
- points: float32 [2, 32768], P(None, ('narrow', 'wide')), may hold values from 0 to 1
- quad_weight: float32 [32768], P(('narrow', 'wide')), may hold values from 9.155274e-06 to 9.1552734e-05
- basis: float32 [4, 2, 32768, 128], P(None, None, ('narrow', 'wide')), may hold values from -6 to 6
- jacobi: float32 [2, 32768], P(None, ('narrow', 'wide')), may hold values from 0.5 to 2
- near_panel: int32 [2048, 12], P(('narrow', 'wide')), may hold values from 0 to 2047, as said below
- near_count: int32 [2048], P(('narrow', 'wide')), may hold values from 2 to 12, as said below
- near_block: bfloat16 [2048, 12, 32, 32], P(('narrow', 'wide')), may hold values from -0.875 to 0.875
- agg_index: int32 [2, 32768], P(None, ('narrow', 'wide')), may hold values from 0 to 47
- coarse_inverse: float32 [8, 1536, 12288], P(None, 'wide', 'narrow'), may hold values from -0.1 to 0.5
Outputs:
- new_block: float32 [2, 32768, 128], P(None, ('narrow', 'wide'))
- hessenberg: float32 [4, 128, 128], replicated
- upper_factor: float32 [128, 128], replicated
The draws below stay inside these ranges and needn't reach their ends.
Inputs may be any that keep to these rules, and one draw needn't show every extreme that they name: near_panel[p, 0] = p; every entry lies within 4 panels of p in panel order, and some entry lies exactly 4 panels away. `near_count`: slots at or beyond a panel's count are not used; some panel uses all 12.
All inputs are finite; a program needn't handle non-finite values.
Results may differ from the reference program's by a relative error of at most 0.0027.
The reference program's roundings to bfloat16 on the way count: a program that leaves them out, or rounds other values in their place, can miss the bound.
Values may be sent and summed in bfloat16 or wider, within the bound.
A program may use at most 64 MiB of HBM per device.

```python
import math
import jax
import jax.numpy as jnp
from jax import lax

Q = 16
NRHS = 128
KB = 4
MAXN = 12
SPAN = 4
CB = 48
PTS_DEV = 128
PANELS = 2048
POINTS = 32768
NC = 12288
N_NARROW = 8


def draw_near_panel(key, part):
    own = jnp.arange(PANELS, dtype=jnp.int32)[:, None]
    slot_index = jnp.arange(MAXN, dtype=jnp.int32)[None, :]
    first_key, second_key, third_key = jax.random.split(jax.random.fold_in(key, 11), 3)
    spread = jax.random.randint(first_key, (PANELS, MAXN), -SPAN, SPAN + 1)
    side_sign = 2 * jax.random.randint(second_key, (PANELS, 1), 0, 2) - 1
    chosen = jax.random.randint(third_key, (), SPAN, PANELS - SPAN)
    offset = jnp.where(slot_index == 0, 0, jnp.where(slot_index == 1, side_sign, spread))
    offset = jnp.where((slot_index == 2) & (own == chosen), SPAN, offset)
    return jnp.clip(own + offset, 0, PANELS - 1).astype(jnp.int32)


def draw_near_count(key, part):
    first_key, second_key = jax.random.split(jax.random.fold_in(key, 23), 2)
    counts = jax.random.randint(first_key, (PANELS,), 2, MAXN + 1)
    chosen = jax.random.randint(second_key, (), 0, PANELS)
    return jnp.where(jnp.arange(PANELS, dtype=jnp.int32) == chosen, MAXN, counts).astype(jnp.int32)


def draw_coarse_inverse(key, part):
    row_span = NC // N_NARROW
    first_key, second_key = jax.random.split(jax.random.fold_in(key, 37), 2)
    shape = (N_NARROW, row_span, NC)
    row_id = jnp.arange(N_NARROW, dtype=jnp.int32)[:, None, None] * row_span + jnp.arange(row_span, dtype=jnp.int32)[None, :, None]
    col_id = jnp.arange(NC, dtype=jnp.int32)[None, None, :]
    spread = jax.random.normal(first_key, shape, jnp.float32) * (0.2 / math.sqrt(NC))
    diagonal = jax.random.uniform(second_key, (N_NARROW, row_span, 1), jnp.float32, 0.1, 0.4)
    return jnp.where(row_id == col_id, diagonal + spread, spread).astype(jnp.float32)


def set_ends(result, stream_key, low, top_value):
    longest = result.shape.index(max(result.shape))
    spots = []
    for shift in (0, 1):
        where = [jax.random.randint(jax.random.fold_in(stream_key, axis), (), 0, length) for axis, length in enumerate(result.shape)]
        where[longest] = (where[longest] + shift) % result.shape[longest]
        spots.append(tuple(where))
    return result.at[spots[0]].set(low).at[spots[1]].set(top_value)


def level_of(own_key, shape, cuts, smallest, top_value):
    loudness, own = 1.0, jax.random.fold_in(own_key, 6)
    for dim, parts in cuts:
        heights = jnp.exp(jax.random.uniform(jax.random.fold_in(own, dim), (parts,), jnp.float32, smallest / len(cuts), top_value / len(cuts)))
        loudness = loudness * jnp.repeat(heights, shape[dim] // parts).reshape([-1 if axis == dim else 1 for axis in range(len(shape))])
    return loudness


def gaussian(own_key, extent, scale, bound, pieces=(), kind=jnp.bfloat16):
    factor_of = level_of(own_key, extent, pieces, -0.22, 0.18) if pieces else 1.0
    values = jax.random.normal(own_key, extent, jnp.float32) * scale * factor_of
    return jnp.minimum(jnp.maximum(values, -bound), bound).astype(kind)


def setup_inputs(seed: int = 0) -> dict:
    arg_keys = jax.random.split(jax.random.key(seed), 10)
    return {
        "points": jnp.clip(1.0 * jax.random.uniform(arg_keys[0], (2, POINTS), jnp.float32) ** level_of(arg_keys[0], (2, POINTS), ((1, 256),), -0.2, 0.2), 0.0, 1.0),
        "quad_weight": jnp.clip(jnp.exp(math.log(9.1552734375e-05) - 2.3025851 * jax.random.uniform(arg_keys[1], (POINTS,), jnp.float32) ** level_of(arg_keys[1], (POINTS,), ((0, 256),), -0.2, 0.2)), 9.15527380129788e-06, 9.1552734375e-05),
        "basis": gaussian(arg_keys[2], (KB, 2, POINTS, NRHS), 0.65, 6.0, ((2, 256),), jnp.float32),
        "jacobi": jnp.clip(jnp.exp(math.log(2.0) - 1.3862944 * jax.random.uniform(arg_keys[3], (2, POINTS), jnp.float32) ** level_of(arg_keys[3], (2, POINTS), ((1, 256),), -0.2, 0.2)), 0.5, 2.0),
        "near_panel": draw_near_panel(jax.random.fold_in(arg_keys[9], 71), 0),
        "near_count": draw_near_count(jax.random.fold_in(arg_keys[9], 71), 0),
        "near_block": gaussian(arg_keys[6], (PANELS, MAXN, 2 * Q, 2 * Q), 0.06, 0.875, ((0, 256),)),
        "agg_index": set_ends(jax.random.randint(arg_keys[7], (2, POINTS), 0, CB), jax.random.fold_in(arg_keys[7], 1), 0, CB - 1).astype(jnp.int32),
        "coarse_inverse": draw_coarse_inverse(jax.random.fold_in(arg_keys[9], 71), 0),
    }


NU = 0.3
DELTA2 = 1e-05
ELASTIC = 40.0
HIGH = lax.Precision.HIGHEST

def far_kernel(targets, sources, weights):
    delta_x = targets[0][:, None] - sources[0][None, :]
    delta_y = targets[1][:, None] - sources[1][None, :]
    square_dist = delta_x * delta_x + delta_y * delta_y + DELTA2
    factor = ELASTIC * weights[None, :]
    log_part = -0.5 * (3.0 - 4.0 * NU) * jnp.log(square_dist)
    g_xx = factor * (log_part + delta_x * delta_x / square_dist)
    g_xy = factor * (delta_x * delta_y / square_dist)
    g_yy = factor * (log_part + delta_y * delta_y / square_dist)
    first_row = jnp.stack([g_xx, g_xy], axis=1)
    second_row = jnp.stack([g_xy, g_yy], axis=1)
    stacked = jnp.stack([first_row, second_row], axis=0)
    return stacked.reshape(2 * targets.shape[1], 2 * sources.shape[1]).astype(jnp.bfloat16)

def reference(points, quad_weight, basis, jacobi, near_panel, near_count, near_block, agg_index, coarse_inverse):
    newest = basis[KB - 1]
    owner = (jnp.arange(POINTS, dtype=jnp.int32) // PTS_DEV).astype(jnp.int32)
    coarse_id = (owner[None, :] * CB + agg_index).astype(jnp.int32)
    coarse_rhs = jax.ops.segment_sum(newest.reshape(2 * POINTS, NRHS), coarse_id.reshape(2 * POINTS), num_segments=NC)
    inverse_full = coarse_inverse.reshape(NC, NC)
    coarse_sol = jnp.dot(inverse_full.astype(jnp.float32), coarse_rhs.astype(jnp.float32), precision=HIGH, preferred_element_type=jnp.float32)
    precond = (jacobi[:, :, None] * newest + coarse_sol[coarse_id]).astype(jnp.bfloat16)
    fields = precond.reshape(2 * POINTS, NRHS).astype(jnp.float32)
    target_size = math.gcd(POINTS, 512)

    def target_block(block_index):
        offset = block_index * target_size
        targets = lax.dynamic_slice_in_dim(points, offset, target_size, 1)
        kernel_rows = far_kernel(targets, points, quad_weight).astype(jnp.float32)
        product = jnp.dot(kernel_rows.astype(jnp.float32), fields.astype(jnp.float32), precision=HIGH, preferred_element_type=jnp.float32)
        return product.reshape(2, target_size, NRHS)
    far_blocks = lax.map(target_block, jnp.arange(POINTS // target_size, dtype=jnp.int32))
    far = jnp.transpose(far_blocks, (1, 0, 2, 3)).reshape(2, POINTS, NRHS)
    panel_fields = precond.reshape(2, PANELS, Q, NRHS)
    gathered = panel_fields[:, near_panel]
    slot_live = jnp.arange(MAXN, dtype=jnp.int32)[None, :] < near_count[:, None]
    gathered = jnp.where(slot_live[None, :, :, None, None], gathered, jnp.zeros((), gathered.dtype))
    gathered = jnp.transpose(gathered, (1, 2, 0, 3, 4)).reshape(PANELS, MAXN, 2 * Q, NRHS)
    near_terms = jnp.einsum('pkxy,pkyr->pxr', near_block.astype(jnp.float32), gathered.astype(jnp.float32), precision=HIGH)
    near = jnp.transpose(near_terms.reshape(PANELS, 2, Q, NRHS), (1, 0, 2, 3)).reshape(2, POINTS, NRHS)
    image = 0.5 * precond.astype(jnp.float32) + far + near
    weighted = basis * quad_weight[None, None, :, None]
    hessenberg = jnp.einsum('jair,aiw->jrw', weighted, image, precision=HIGH)
    remainder = image - jnp.einsum('jair,jrw->aiw', basis, hessenberg, precision=HIGH)
    gram_matrix = jnp.einsum('air,aiw->rw', remainder * quad_weight[None, :, None], remainder, precision=HIGH)
    lower_factor = jnp.linalg.cholesky(gram_matrix)
    flat = remainder.reshape(2 * POINTS, NRHS)
    solved = jax.scipy.linalg.solve_triangular(lower_factor, flat.T, lower=True)
    new_block = solved.T.reshape(2, POINTS, NRHS)
    return (new_block, hessenberg, lower_factor.T)
```

```python
import functools
import math

import jax
import jax.numpy as jnp
from jax import lax
from jax.experimental import pallas as pl
from jax.experimental.pallas import tpu as pltpu
from jax.sharding import PartitionSpec as P

SPAN = 4


NU = 0.3
DELTA2 = 1e-05
ELASTIC = 40.0
HIGH = lax.Precision.HIGHEST


def extended(block, sides, width):
    for axis, dim in sides:
        count = lax.axis_size(axis)
        forward = [(i, i + 1) for i in range(count - 1)]
        backward = [(target, source) for source, target in forward]
        low = lax.ppermute(
            lax.slice_in_dim(block, block.shape[dim] - width, None, axis=dim), axis, forward
        )
        high = lax.ppermute(lax.slice_in_dim(block, 0, width, axis=dim), axis, backward)
        block = jnp.concatenate([low, block, high], axis=dim)
    return block


def far_kernel(targets, sources, weights):
    delta_x = targets[0][:, None] - sources[0][None, :]
    delta_y = targets[1][:, None] - sources[1][None, :]
    square_dist = delta_x * delta_x + delta_y * delta_y + DELTA2
    factor = ELASTIC * weights[None, :]
    log_part = -0.5 * (3.0 - 4.0 * NU) * jnp.log(square_dist)
    g_xx = factor * (log_part + delta_x * delta_x / square_dist)
    g_xy = factor * (delta_x * delta_y / square_dist)
    g_yy = factor * (log_part + delta_y * delta_y / square_dist)
    first_row = jnp.stack([g_xx, g_xy], axis=1)
    second_row = jnp.stack([g_xy, g_yy], axis=1)
    stacked = jnp.stack([first_row, second_row], axis=0)
    return stacked.reshape(2 * targets.shape[1], 2 * sources.shape[1]).astype(jnp.bfloat16)


def far_product(targets, sources, weights, fields):
    piece_len = sources.shape[1]
    row_count = targets.shape[1]
    rhs_count = fields.shape[2]
    block_size = math.gcd(piece_len, max(512, 524288 // row_count))
    block_count = piece_len // block_size

    def one_block(block_index, running):
        offset = block_index * block_size
        source_block = lax.dynamic_slice_in_dim(sources, offset, block_size, 1)
        weight_block = lax.dynamic_slice_in_dim(weights, offset, block_size, 0)
        field_block = lax.dynamic_slice_in_dim(fields, offset, block_size, 1)
        kernel_block = far_kernel(targets, source_block, weight_block)
        return running + jnp.dot(
            kernel_block,
            field_block.reshape(2 * block_size, rhs_count),
            preferred_element_type=jnp.float32,
        )

    initial = jnp.zeros((2 * row_count, rhs_count), jnp.float32)
    return lax.fori_loop(0, block_count, one_block, initial)


def make_fold(targets, source_all, shard_piece):
    return far_product(targets, source_all[0:2], source_all[2], shard_piece)


MESH = pl.DeviceIdType.MESH
NZ = 8
PANEL = 16


def mm(a, b, dims):
    return lax.dot_general(a, b, (dims, ((), ())), precision=HIGH, preferred_element_type=jnp.float32)


def swap(count, me, device, src, dst, sems, go):
    def one(k, carry):
        peer = lax.rem(me + k, count)
        copy = pltpu.make_async_remote_copy(
            src_ref=src(peer),
            dst_ref=dst,
            send_sem=sems.at[0, k],
            recv_sem=sems.at[1, k],
            device_id=device(peer),
            device_id_type=MESH,
        )
        if go:
            copy.start()
        else:
            copy.wait()
        return carry

    lax.fori_loop(1, count, one, 0)


def exchange(count, me, device, src, dst, sems):
    swap(count, me, device, src, dst, sems, True)
    swap(count, me, device, src, dst, sems, False)


def slots_sum(ref, count):
    total = ref[0]
    for k in range(1, count):
        total = total + ref[k]
    return total


def greet(nn, nw, n, w):
    barrier = pltpu.get_barrier_semaphore()

    def wide_one(k, carry):
        pl.semaphore_signal(barrier, inc=1, device_id={"wide": lax.rem(w + k, nw)}, device_id_type=MESH)
        return carry

    def narrow_one(k, carry):
        pl.semaphore_signal(barrier, inc=1, device_id={"narrow": lax.rem(n + k, nn)}, device_id_type=MESH)
        return carry

    lax.fori_loop(1, nw, wide_one, 0)
    lax.fori_loop(1, nn, narrow_one, 0)
    pl.semaphore_wait(barrier, nw + nn - 2)


def factor(gram, work):
    size = gram.shape[0]
    rows = lax.broadcasted_iota(jnp.int32, (size, size), 0)
    cols = lax.broadcasted_iota(jnp.int32, (size, size), 1)
    work[:, 0:size] = gram
    work[:, size:] = (rows == cols).astype(jnp.float32)
    sub = lax.broadcasted_iota(jnp.int32, (PANEL, 1), 0)
    for base in range(0, size, PANEL):
        panel = work[base : base + PANEL, :]
        for k in range(PANEL):
            pivot = panel[k : k + 1, base + k : base + k + 1]
            row = panel[k : k + 1, :] * lax.rsqrt(pivot)
            left = panel[:, base + k : base + k + 1] * lax.rsqrt(pivot)
            panel = jnp.where(sub == k, row, jnp.where(sub > k, panel - left * row, panel))
        work[base : base + PANEL, :] = panel
        if base + PANEL < size:
            below = mm(panel[:, 0:size], panel, ((0,), (0,)))
            work[base + PANEL :, :] = work[base + PANEL :, :] - below[base + PANEL :, :]


def tail_kernel(
    nn, nw, nz,
    weight_ref, basis_ref, image_ref,
    new_ref, hess_ref, upper_ref,
    send_h, slots_h, mid_h, slots_n, full_h,
    send_g, slots_gz, mid_g, slots_gx, mid_g2, slots_gn, mid_g3, full_g,
    rest, work,
    sems_w, sems_n, sems_w2, sems_z, sems_x, sems_gn, sems_z2,
):
    n = lax.axis_index("narrow")
    w = lax.axis_index("wide")
    x, z = w // nz, lax.rem(w, nz)
    nx = nw // nz
    blocks, size = basis_ref.shape[0], image_ref.shape[1]
    points = weight_ref.shape[1]
    greet(nn, nw, n, w)

    def wide_peer(p):
        return {"wide": p}

    def narrow_peer(p):
        return {"narrow": p}

    def z_peer(p):
        return {"wide": x * nz + p}

    def x_peer(p):
        return {"wide": p * nz + z}

    spread = jnp.transpose(jnp.broadcast_to(weight_ref[...], (points, points)))
    scale = jnp.concatenate([spread, spread], axis=0)
    image = image_ref[...]
    weighted = image * scale
    for j in range(blocks):
        send_h[j * size : (j + 1) * size, :] = mm(basis_ref[j], weighted, ((0,), (0,)))
    step = blocks * size // nw

    def chunk(ref, p, rows):
        return ref.at[pl.ds(pl.multiple_of(p * rows, rows), rows), :]

    swap(nw, w, wide_peer, lambda p: chunk(send_h, p, step), slots_h.at[w], sems_w, True)
    slots_h[w] = send_h[pl.ds(pl.multiple_of(w * step, step), step), :]
    swap(nw, w, wide_peer, lambda p: chunk(send_h, p, step), slots_h.at[w], sems_w, False)
    mid_h[...] = slots_sum(slots_h, nw)
    swap(nn, n, narrow_peer, lambda p: mid_h, slots_n.at[n], sems_n, True)
    slots_n[n] = mid_h[...]
    swap(nn, n, narrow_peer, lambda p: mid_h, slots_n.at[n], sems_n, False)
    mine = slots_sum(slots_n, nn)
    full_h[pl.ds(pl.multiple_of(w * step, step), step), :] = mine
    exchange(nw, w, wide_peer, lambda p: chunk(full_h, w, step), chunk(full_h, w, step), sems_w2)
    remainder = image
    for j in range(blocks):
        part = full_h[j * size : (j + 1) * size, :]
        hess_ref[j] = part
        remainder = remainder - mm(basis_ref[j], part, ((1,), (0,)))
    rest[...] = remainder
    send_g[...] = mm(remainder * scale, remainder, ((0,), (0,)))
    gstep = size // nz
    swap(nz, z, z_peer, lambda p: chunk(send_g, p, gstep), slots_gz.at[z], sems_z, True)
    slots_gz[z] = send_g[pl.ds(pl.multiple_of(z * gstep, gstep), gstep), :]
    swap(nz, z, z_peer, lambda p: chunk(send_g, p, gstep), slots_gz.at[z], sems_z, False)
    mid_g[...] = slots_sum(slots_gz, nz)
    swap(nx, x, x_peer, lambda p: mid_g, slots_gx.at[x], sems_x, True)
    slots_gx[x] = mid_g[...]
    swap(nx, x, x_peer, lambda p: mid_g, slots_gx.at[x], sems_x, False)
    mid_g2[...] = slots_sum(slots_gx, nx)
    swap(nn, n, narrow_peer, lambda p: mid_g2, slots_gn.at[n], sems_gn, True)
    slots_gn[n] = mid_g2[...]
    swap(nn, n, narrow_peer, lambda p: mid_g2, slots_gn.at[n], sems_gn, False)
    full_g[pl.ds(pl.multiple_of(z * gstep, gstep), gstep), :] = slots_sum(slots_gn, nn)
    exchange(nz, z, z_peer, lambda p: chunk(full_g, z, gstep), chunk(full_g, z, gstep), sems_z2)
    factor(full_g[...], work)
    row = lax.broadcasted_iota(jnp.int32, (size, size), 0)
    col = lax.broadcasted_iota(jnp.int32, (size, size), 1)
    upper_ref[...] = jnp.where(row <= col, work[:, 0:size], 0.0)
    new_ref[...] = mm(rest[...], work[:, size:], ((1,), (1,)))


def tail(weight, basis, image, nn, nw, nz):
    blocks, rows, size = basis.shape
    f32 = jnp.float32
    vmem = pl.BlockSpec(memory_space=pltpu.VMEM)
    step, gstep, nx = blocks * size // nw, size // nz, nw // nz
    dma = lambda c: pltpu.SemaphoreType.DMA((2, c))
    return pl.pallas_call(
        functools.partial(tail_kernel, nn, nw, nz),
        name="tail",
        out_shape=(
            jax.ShapeDtypeStruct((rows, size), f32),
            jax.ShapeDtypeStruct((blocks, size, size), f32),
            jax.ShapeDtypeStruct((size, size), f32),
        ),
        in_specs=[vmem] * 3,
        out_specs=(vmem,) * 3,
        scratch_shapes=[
            pltpu.VMEM((blocks * size, size), f32),
            pltpu.VMEM((nw, step, size), f32),
            pltpu.VMEM((step, size), f32),
            pltpu.VMEM((nn, step, size), f32),
            pltpu.VMEM((blocks * size, size), f32),
            pltpu.VMEM((size, size), f32),
            pltpu.VMEM((nz, gstep, size), f32),
            pltpu.VMEM((gstep, size), f32),
            pltpu.VMEM((nx, gstep, size), f32),
            pltpu.VMEM((gstep, size), f32),
            pltpu.VMEM((nn, gstep, size), f32),
            pltpu.VMEM((gstep, size), f32),
            pltpu.VMEM((size, size), f32),
            pltpu.VMEM((rows, size), f32),
            pltpu.VMEM((size, 2 * size), f32),
            dma(nw), dma(nn), dma(nw), dma(nz), dma(nx), dma(nn), dma(nz),
        ],
        compiler_params=pltpu.CompilerParams(collective_id=0, has_side_effects=True),
    )(weight, basis, image)


def body(
    points,
    quad_weight,
    basis,
    jacobi,
    near_panel,
    near_count,
    near_block,
    agg_index,
    coarse_inverse,
):
    block_total = basis.shape[0]
    point_count = basis.shape[2]
    rhs_count = basis.shape[3]
    coarse_count = coarse_inverse.shape[1]
    newest = basis[block_total - 1]
    member = (
        agg_index[:, :, None] == jnp.arange(coarse_count, dtype=jnp.int32)[None, None, :]
    ).astype(jnp.float32)
    coarse_rhs = jnp.einsum("apc,apr->cr", member, newest, precision=HIGH)
    coarse_part = jnp.einsum(
        "abc,cr->abr",
        coarse_inverse,
        lax.all_gather(coarse_rhs, "wide", axis=0, tiled=True),
        precision=HIGH,
    )
    coarse_sol = lax.psum_scatter(coarse_part, "narrow", scatter_dimension=0, tiled=True)[0]
    lifted = jnp.einsum("apc,cr->apr", member, coarse_sol, precision=HIGH)
    precond = (jacobi[:, :, None] * newest + lifted).astype(jnp.bfloat16)
    source_info = jnp.concatenate([points, quad_weight[None, :]], axis=0)
    targets = lax.all_gather(points, "narrow", axis=1, tiled=True)
    source_all = lax.all_gather(source_info, "wide", axis=1, tiled=True)
    far_part = make_fold(targets, source_all, lax.all_gather(precond, "wide", axis=1, tiled=True))
    far_local = lax.psum_scatter(
        far_part.reshape(2, targets.shape[1], rhs_count), "narrow", scatter_dimension=1, tiled=True
    )
    panels_dev = near_panel.shape[0]
    slot_total = near_panel.shape[1]
    nodes = near_block.shape[2] // 2
    padded = extended(precond, ((("narrow", "wide"), 1),), SPAN * nodes)
    panel_fields = padded.reshape(2, panels_dev + 2 * SPAN, nodes, rhs_count)
    local_index = near_panel - lax.axis_index(("narrow", "wide")) * panels_dev + SPAN
    gathered = panel_fields[:, local_index]
    slot_live = jnp.arange(slot_total, dtype=jnp.int32)[None, :] < near_count[:, None]
    gathered = jnp.where(slot_live[None, :, :, None, None], gathered, jnp.zeros((), gathered.dtype))
    gathered = jnp.transpose(gathered, (1, 2, 0, 3, 4)).reshape(
        panels_dev, slot_total, 2 * nodes, rhs_count
    )
    near_terms = jnp.einsum(
        "pkxy,pkyr->pxr", near_block, gathered, preferred_element_type=jnp.float32
    )
    near = jnp.transpose(near_terms.reshape(panels_dev, 2, nodes, rhs_count), (1, 0, 2, 3)).reshape(
        2, point_count, rhs_count
    )
    image = 0.5 * precond.astype(jnp.float32) + far_local + near
    new_flat, hessenberg, upper = tail(
        quad_weight[None, :],
        basis.reshape(block_total, 2 * point_count, rhs_count),
        image.reshape(2 * point_count, rhs_count),
        lax.axis_size("narrow"),
        lax.axis_size("wide"),
        NZ,
    )
    return (new_flat.reshape(2, point_count, rhs_count), hessenberg, upper)


def solution(mesh):
    in_specs = (
        P(None, ("narrow", "wide")),
        P(("narrow", "wide")),
        P(None, None, ("narrow", "wide"), None),
        P(None, ("narrow", "wide")),
        P(("narrow", "wide"), None),
        P(("narrow", "wide")),
        P(("narrow", "wide"), None, None, None),
        P(None, ("narrow", "wide")),
        P(None, "wide", "narrow"),
    )
    out_specs = (P(None, ("narrow", "wide"), None), P(), P())
    return jax.shard_map(body, mesh=mesh, in_specs=in_specs, out_specs=out_specs, check_vma=False)
```

```python
import functools

import jax
import jax.numpy as jnp
from jax import lax
from jax.experimental import pallas as pl
from jax.experimental.pallas import tpu as pltpu
from jax.sharding import PartitionSpec as P

NU = 0.3
DELTA2 = 1e-05
ELASTIC = 40.0
HIGH = lax.Precision.HIGHEST
MESH = pl.DeviceIdType.MESH
NZ = 8
PANEL = 16
HALF = 64


def mm(a, b, dims):
    return lax.dot_general(a, b, (dims, ((), ())), precision=HIGH, preferred_element_type=jnp.float32)


def swap(count, me, device, src, dst, sems, go):
    def one(k, carry):
        peer = lax.rem(me + k, count)
        copy = pltpu.make_async_remote_copy(
            src_ref=src(peer),
            dst_ref=dst,
            send_sem=sems.at[0, k],
            recv_sem=sems.at[1, k],
            device_id=device(peer),
            device_id_type=MESH,
        )
        if go:
            copy.start()
        else:
            copy.wait()
        return carry

    lax.fori_loop(1, count, one, 0)


def exchange(count, me, device, src, dst, sems):
    swap(count, me, device, src, dst, sems, True)
    swap(count, me, device, src, dst, sems, False)


def ring(count, me, device, block, half, sems, step, go):
    back = step - 1
    for way, peer, origin in ((0, me + 1, me + count - back), (1, me + count - 1, me + back)):
        peer, origin = lax.rem(peer, count), lax.rem(origin, count)
        ref = half(origin, way) if step == count // 2 else block(origin)
        copy = pltpu.make_async_remote_copy(
            src_ref=ref,
            dst_ref=ref,
            send_sem=sems.at[0, way, back],
            recv_sem=sems.at[1, way, back],
            device_id=device(peer),
            device_id_type=MESH,
        )
        if go:
            copy.start()
        else:
            copy.wait()


def slots_sum(ref, count):
    total = ref[0]
    for k in range(1, count):
        total = total + ref[k]
    return total


def greet(nn, nw, n, w, before, after):
    barrier = pltpu.get_barrier_semaphore()

    def wide_one(k, carry):
        pl.semaphore_signal(barrier, inc=1, device_id={"wide": lax.rem(w + k, nw)}, device_id_type=MESH)
        return carry

    def narrow_one(k, carry):
        pl.semaphore_signal(barrier, inc=1, device_id={"narrow": lax.rem(n + k, nn)}, device_id_type=MESH)
        return carry

    lax.fori_loop(1, nw, wide_one, 0)
    lax.fori_loop(1, nn, narrow_one, 0)
    for peer in (before, after):
        pl.semaphore_signal(barrier, inc=1, device_id=peer, device_id_type=MESH)
    pl.semaphore_wait(barrier, nw + nn)


def factor(gram, work):
    size = gram.shape[0]
    rows = lax.broadcasted_iota(jnp.int32, (size, size), 0)
    cols = lax.broadcasted_iota(jnp.int32, (size, size), 1)
    work[:, 0:size] = gram
    work[:, size:] = (rows == cols).astype(jnp.float32)
    sub = lax.broadcasted_iota(jnp.int32, (PANEL, 1), 0)
    for base in range(0, size, PANEL):
        panel = work[base : base + PANEL, :]
        for k in range(PANEL):
            pivot = panel[k : k + 1, base + k : base + k + 1]
            row = panel[k : k + 1, :] * lax.rsqrt(pivot)
            left = panel[:, base + k : base + k + 1] * lax.rsqrt(pivot)
            panel = jnp.where(sub == k, row, jnp.where(sub > k, panel - left * row, panel))
        work[base : base + PANEL, :] = panel
        if base + PANEL < size:
            below = mm(panel[:, 0:size], panel, ((0,), (0,)))
            work[base + PANEL :, :] = work[base + PANEL :, :] - below[base + PANEL :, :]


def column(row, points):
    return jnp.transpose(jnp.broadcast_to(row, (points, points)))


def step_kernel(
    nn, nw, nz,
    panel_ref, count_ref, points_ref, weight_ref, basis_ref, jacobi_ref, agg_ref, block_ref, inverse_ref,
    new_ref, hess_ref, upper_ref,
    info, info_w, info_n, sources, columns, green,
    rhs_all, parts, part_slots, fields_a, fields_b, window, halo, far, far_slots, near,
    send_h, slots_h, mid_h, slots_n, full_h,
    send_g, slots_gz, mid_g, slots_gx, mid_g2, slots_gn, full_g,
    rest, work,
    sems_iw, sems_in, sems_cx, sems_cz, sems_cn, sems_halo,
    sems_ax, sems_az, sems_bz, sems_bx, sems_far,
    sems_w, sems_n, sems_w2, sems_z, sems_x, sems_gn, sems_z2,
):
    f32, bf16 = jnp.float32, jnp.bfloat16
    n = lax.axis_index("narrow")
    w = lax.axis_index("wide")
    x, z = w // nz, lax.rem(w, nz)
    nx = nw // nz
    blocks, size = basis_ref.shape[0], basis_ref.shape[2]
    points = weight_ref.shape[1]
    coarse = inverse_ref.shape[1]
    flat = n * nw + w
    total = nn * nw

    def flat_peer(p):
        return {"narrow": p // nw, "wide": lax.rem(p, nw)}

    before, after = flat_peer(lax.rem(flat + total - 1, total)), flat_peer(lax.rem(flat + 1, total))
    greet(nn, nw, n, w, before, after)

    def wide_peer(p):
        return {"wide": p}

    def narrow_peer(p):
        return {"narrow": p}

    def z_peer(p):
        return {"wide": x * nz + p}

    def x_peer(p):
        return {"wide": p * nz + z}

    info[...] = jnp.zeros_like(info)
    info[0:2, :] = points_ref[...]
    info[2:3, :] = ELASTIC * weight_ref[...]
    swap(nn, n, narrow_peer, lambda p: info, info_n.at[n], sems_in, True)
    swap(nw, w, wide_peer, lambda p: info, info_w.at[w], sems_iw, True)
    info_n[n] = info[...]
    info_w[w] = info[...]

    ids = lax.broadcasted_iota(jnp.int32, (coarse, points), 0)
    member = [(ids == agg_ref[a : a + 1, :]).astype(f32) for a in range(2)]
    newest = [basis_ref[blocks - 1, a * points : (a + 1) * points, :] for a in range(2)]
    rhs_all[x, z] = mm(member[0], newest[0], ((1,), (0,))) + mm(member[1], newest[1], ((1,), (0,)))
    swap(nx, x, x_peer, lambda p: rhs_all.at[x, z], rhs_all.at[x, z], sems_cx, True)

    def rhs_ring(step, go):
        ring(
            nz, z, z_peer,
            lambda p: rhs_all.at[:, p],
            lambda p, way: rhs_all.at[pl.ds(way * (nx // 2), nx // 2), p],
            sems_cz, step, go,
        )

    swap(nx, x, x_peer, lambda p: rhs_all.at[x, z], rhs_all.at[x, z], sems_cx, False)
    rhs_ring(1, True)

    swap(nn, n, narrow_peer, lambda p: info, info_n.at[n], sems_in, False)
    swap(nw, w, wide_peer, lambda p: info, info_w.at[w], sems_iw, False)
    lane = lax.broadcasted_iota(jnp.int32, (8, points), 1)
    pairs = nx // 2
    for p in range(nz):
        for m in range(pairs):
            one, two = info_w[(2 * m) * nz + p], info_w[(2 * m + 1) * nz + p]
            sources[p, m] = jnp.where(lane < HALF, one, pltpu.roll(two, HALF, 1))
    for p in range(nx):
        for h in range(2):
            for m in range(pairs):
                at = p * nz + h * (nz // 2) + 2 * m
                one, two = info_w[at], info_w[at + 1]
                sources[nz + 2 * p + h, m] = jnp.where(lane < HALF, pltpu.roll(one, HALF, 1), two)
    for t in range(nn):
        tile = info_n[t]
        for a in range(2):
            columns[t, a] = column(tile[a : a + 1, :], points)

    chunks = nz + 2 * nx
    tall = 32

    def evaluate(first, last):
        def unit(i, carry):
            c, t = i // nn, lax.rem(i, nn)
            for m in range(pairs):
                src = sources[c, m]
                sx, sy, sw = src[0:1, :], src[1:2, :], src[2:3, :]
                for r in range(0, points, tall):
                    dx = columns[t, 0, r : r + tall, :] - sx
                    dy = columns[t, 1, r : r + tall, :] - sy
                    xx, yy = dx * dx, dy * dy
                    square = xx + yy + DELTA2
                    inv = 1.0 / square
                    log_part = (-0.5 * (3.0 - 4.0 * NU)) * jnp.log(square)
                    rows = pl.ds(pl.multiple_of(t * points + r, tall), tall)
                    cols = slice(m * points, (m + 1) * points)
                    green[c, 0, rows, cols] = (sw * (log_part + xx * inv)).astype(bf16)
                    green[c, 1, rows, cols] = (sw * (dx * dy * inv)).astype(bf16)
                    green[c, 2, rows, cols] = (sw * (log_part + yy * inv)).astype(bf16)
            return carry

        lax.fori_loop(first * nn, last * nn, unit, 0)

    done = 0
    for step in range(1, nz // 2 + 1):
        evaluate(done, done + chunks // 8)
        done += chunks // 8
        rhs_ring(step, False)
        if step < nz // 2:
            rhs_ring(step + 1, True)

    inverse = inverse_ref[...].reshape(nn * coarse, nw * coarse)
    parts[...] = mm(inverse, rhs_all[...].reshape(nw * coarse, size), ((1,), (0,))).reshape(nn, coarse, size)
    swap(nn, n, narrow_peer, lambda p: parts.at[p], part_slots.at[n], sems_cn, True)
    part_slots[n] = parts[n]
    evaluate(done, done + chunks // 4)
    done += chunks // 4
    swap(nn, n, narrow_peer, lambda p: parts.at[p], part_slots.at[n], sems_cn, False)
    sol = slots_sum(part_slots, nn)
    for a in range(2):
        lifted = mm(member[a], sol, ((0,), (0,)))
        field = (column(jacobi_ref[a : a + 1, :], points) * newest[a] + lifted).astype(bf16)
        window[HALF : HALF + points, a * size : (a + 1) * size] = field
    fields_a[z, x] = window[HALF : 2 * HALF, :]
    fields_b[x, z] = window[2 * HALF : 3 * HALF, :]

    lanes = max(nx // 2, 1)

    def a_ring(step, go):
        for j in range(lanes):
            ring(
                nz, z, z_peer,
                lambda p: fields_a.at[p, 2 * j : 2 * j + 2],
                lambda p, way: fields_a.at[p, 2 * j + way],
                sems_az.at[j], step, go,
            )

    def b_ring(step, go):
        ring(
            nz, z, z_peer,
            lambda p: fields_b.at[x, p],
            lambda p, way: fields_b.at[x, p, way * (HALF // 2) : (way + 1) * (HALF // 2)],
            sems_bz, step, go,
        )

    def bx_ring(step, go):
        q = nz // 4
        for j in range(2):
            ring(
                nx, x, x_peer,
                lambda p: fields_b.at[p, 2 * q * j : 2 * q * (j + 1)],
                lambda p, way: fields_b.at[p, 2 * q * j + q * way : 2 * q * j + q * (way + 1)],
                sems_bx.at[j], step, go,
            )

    def halo_copy(way, src, peer, go):
        copy = pltpu.make_async_remote_copy(
            src_ref=src, dst_ref=halo.at[way], send_sem=sems_halo.at[0, way], recv_sem=sems_halo.at[1, way],
            device_id=peer, device_id_type=MESH,
        )
        if go:
            copy.start()
        else:
            copy.wait()

    def halos(go):
        halo_copy(0, fields_b.at[x, z], after, go)
        halo_copy(1, fields_a.at[z, x], before, go)

    def a_first(go):
        swap(nx, x, x_peer, lambda p: fields_a.at[z, x], fields_a.at[z, x], sems_ax, go)

    a_first(True)
    b_ring(1, True)
    halos(True)

    def accumulate(c, field, first):
        left, right = field[:, 0:size], field[:, size:]

        def rows_of(i, carry):
            rows = pl.ds(pl.multiple_of(i * 2 * points, 2 * points), 2 * points)
            cross = jnp.dot(green[c, 1, rows, :], field, preferred_element_type=f32)
            one = jnp.dot(green[c, 0, rows, :], left, preferred_element_type=f32) + cross[:, size:]
            two = jnp.dot(green[c, 2, rows, :], right, preferred_element_type=f32) + cross[:, 0:size]
            if first:
                far[rows, 0:size] = one
                far[rows, size:] = two
            else:
                far[rows, 0:size] = far[rows, 0:size] + one
                far[rows, size:] = far[rows, size:] + two
            return carry

        lax.fori_loop(0, nn // 2, rows_of, 0)

    def take_a(p, first=False):
        p = lax.rem(p, nz)
        accumulate(p, fields_a[p].reshape(nx * HALF, 2 * size), first)

    def take_b(p):
        p = lax.rem(p, nx)
        for h in range(2):
            part = fields_b[p, h * (nz // 2) : (h + 1) * (nz // 2)]
            accumulate(nz + 2 * p + h, part.reshape(nz // 2 * HALF, 2 * size), False)

    evaluate(done, done + 1)
    done += 1
    a_first(False)
    a_ring(1, True)
    b_ring(1, False)
    if nz // 2 > 1:
        b_ring(2, True)
    evaluate(done, chunks)
    take_a(z, True)

    def near_field():
        halos(False)
        window[0:HALF, :] = halo[0]
        window[HALF + points :, :] = halo[1]
        q = block_ref.shape[2] // 2
        panels, slots = block_ref.shape[0], block_ref.shape[1]

        reach = points + 2 * HALF
        row_id = lax.broadcasted_iota(jnp.int32, (q, reach), 0)
        col_id = lax.broadcasted_iota(jnp.int32, (q, reach), 1)

        def one_panel(p, carry):
            live = jnp.full((q, reach), count_ref[p], jnp.int32)
            picks = []
            for k in range(slots):
                start = jnp.full((q, reach), (panel_ref[p, k] - flat * panels) * q + HALF, jnp.int32)
                picks.append(((col_id == start + row_id) & (live > k)).astype(f32))
            pick = jnp.concatenate(picks, axis=0).astype(bf16)
            rows = jnp.dot(pick, window[...], preferred_element_type=f32).astype(bf16)
            total = jnp.zeros((2 * q, size), f32)
            for k in range(slots):
                one = rows[k * q : (k + 1) * q, :]
                both = jnp.concatenate([one[:, 0:size], one[:, size:]], axis=0)
                total = total + jnp.dot(block_ref[p, k], both, preferred_element_type=f32)
            for a in range(2):
                near[pl.ds(pl.multiple_of(a * points + p * q, q), q), :] = total[a * q : (a + 1) * q, :]
            return carry

        lax.fori_loop(0, panels, one_panel, 0)

    for step in range(1, nz // 2 + 1):
        a_ring(step, False)
        if step < nz // 2:
            a_ring(step + 1, True)
            b_ring(step + 1, False)
            if step + 2 <= nz // 2:
                b_ring(step + 2, True)
            else:
                bx_ring(1, True)
        if step == 1:
            near_field()
        take_a(z + nz - step)
        if step < nz // 2:
            take_a(z + step)
    take_b(x)
    for step in range(1, nx // 2 + 1):
        bx_ring(step, False)
        if step < nx // 2:
            bx_ring(step + 1, True)
        take_b(x + nx - step)
        if step < nx // 2:
            take_b(x + step)

    def target(p):
        return far.at[pl.ds(pl.multiple_of(p * points, points), points), :]

    swap(nn, n, narrow_peer, target, far_slots.at[n], sems_far, True)
    far_slots[n] = far[pl.ds(pl.multiple_of(n * points, points), points), :]
    swap(nn, n, narrow_peer, target, far_slots.at[n], sems_far, False)
    far_sum = slots_sum(far_slots, nn)
    image = jnp.concatenate(
        [
            0.5 * window[HALF : HALF + points, a * size : (a + 1) * size].astype(f32)
            + far_sum[:, a * size : (a + 1) * size]
            + near[a * points : (a + 1) * points, :]
            for a in range(2)
        ],
        axis=0,
    )

    spread = column(weight_ref[...], points)
    scale = jnp.concatenate([spread, spread], axis=0)
    weighted = image * scale
    for j in range(blocks):
        send_h[j * size : (j + 1) * size, :] = mm(basis_ref[j], weighted, ((0,), (0,)))
    step = blocks * size // nw

    def chunk(ref, p, rows):
        return ref.at[pl.ds(pl.multiple_of(p * rows, rows), rows), :]

    swap(nw, w, wide_peer, lambda p: chunk(send_h, p, step), slots_h.at[w], sems_w, True)
    slots_h[w] = send_h[pl.ds(pl.multiple_of(w * step, step), step), :]
    swap(nw, w, wide_peer, lambda p: chunk(send_h, p, step), slots_h.at[w], sems_w, False)
    mid_h[...] = slots_sum(slots_h, nw)
    swap(nn, n, narrow_peer, lambda p: mid_h, slots_n.at[n], sems_n, True)
    slots_n[n] = mid_h[...]
    swap(nn, n, narrow_peer, lambda p: mid_h, slots_n.at[n], sems_n, False)
    full_h[pl.ds(pl.multiple_of(w * step, step), step), :] = slots_sum(slots_n, nn)
    exchange(nw, w, wide_peer, lambda p: chunk(full_h, w, step), chunk(full_h, w, step), sems_w2)
    remainder = image
    for j in range(blocks):
        part = full_h[j * size : (j + 1) * size, :]
        hess_ref[j] = part
        remainder = remainder - mm(basis_ref[j], part, ((1,), (0,)))
    rest[...] = remainder
    send_g[...] = mm(remainder * scale, remainder, ((0,), (0,)))
    gstep = size // nz
    swap(nz, z, z_peer, lambda p: chunk(send_g, p, gstep), slots_gz.at[z], sems_z, True)
    slots_gz[z] = send_g[pl.ds(pl.multiple_of(z * gstep, gstep), gstep), :]
    swap(nz, z, z_peer, lambda p: chunk(send_g, p, gstep), slots_gz.at[z], sems_z, False)
    mid_g[...] = slots_sum(slots_gz, nz)
    swap(nx, x, x_peer, lambda p: mid_g, slots_gx.at[x], sems_x, True)
    slots_gx[x] = mid_g[...]
    swap(nx, x, x_peer, lambda p: mid_g, slots_gx.at[x], sems_x, False)
    mid_g2[...] = slots_sum(slots_gx, nx)
    swap(nn, n, narrow_peer, lambda p: mid_g2, slots_gn.at[n], sems_gn, True)
    slots_gn[n] = mid_g2[...]
    swap(nn, n, narrow_peer, lambda p: mid_g2, slots_gn.at[n], sems_gn, False)
    full_g[pl.ds(pl.multiple_of(z * gstep, gstep), gstep), :] = slots_sum(slots_gn, nn)
    exchange(nz, z, z_peer, lambda p: chunk(full_g, z, gstep), chunk(full_g, z, gstep), sems_z2)
    factor(full_g[...], work)
    row = lax.broadcasted_iota(jnp.int32, (size, size), 0)
    col = lax.broadcasted_iota(jnp.int32, (size, size), 1)
    upper_ref[...] = jnp.where(row <= col, work[:, 0:size], 0.0)
    new_ref[...] = mm(rest[...], work[:, size:], ((1,), (1,)))


def whole_step(panel, count, points, weight, basis, jacobi, agg, block, inverse, nn, nw, nz):
    blocks, rows, size = basis.shape
    f32, bf16 = jnp.float32, jnp.bfloat16
    pts = weight.shape[1]
    coarse = inverse.shape[1]
    vmem = pl.BlockSpec(memory_space=pltpu.VMEM)
    smem = pl.BlockSpec(memory_space=pltpu.SMEM)
    step, gstep, nx = blocks * size // nw, size // nz, nw // nz
    chunks, cols = nz + 2 * nx, nx * HALF
    dma = lambda *c: pltpu.SemaphoreType.DMA((2, *c))
    lanes = max(nx // 2, 1)
    buf = pltpu.VMEM
    return pl.pallas_call(
        functools.partial(step_kernel, nn, nw, nz),
        name="step",
        out_shape=(
            jax.ShapeDtypeStruct((rows, size), f32),
            jax.ShapeDtypeStruct((blocks, size, size), f32),
            jax.ShapeDtypeStruct((size, size), f32),
        ),
        in_specs=[smem] * 2 + [vmem] * 7,
        out_specs=(vmem,) * 3,
        scratch_shapes=[
            buf((8, pts), f32),
            buf((nw, 8, pts), f32),
            buf((nn, 8, pts), f32),
            buf((chunks, nx // 2, 8, pts), f32),
            buf((nn, 2, pts, pts), f32),
            buf((chunks, 3, nn * pts, cols), bf16),
            buf((nx, nz, coarse, size), f32),
            buf((nn, coarse, size), f32),
            buf((nn, coarse, size), f32),
            buf((nz, nx, HALF, 2 * size), bf16),
            buf((nx, nz, HALF, 2 * size), bf16),
            buf((pts + 2 * HALF, 2 * size), bf16),
            buf((2, HALF, 2 * size), bf16),
            buf((nn * pts, 2 * size), f32),
            buf((nn, pts, 2 * size), f32),
            buf((rows, size), f32),
            buf((blocks * size, size), f32),
            buf((nw, step, size), f32),
            buf((step, size), f32),
            buf((nn, step, size), f32),
            buf((blocks * size, size), f32),
            buf((size, size), f32),
            buf((nz, gstep, size), f32),
            buf((gstep, size), f32),
            buf((nx, gstep, size), f32),
            buf((gstep, size), f32),
            buf((nn, gstep, size), f32),
            buf((size, size), f32),
            buf((rows, size), f32),
            buf((size, 2 * size), f32),
            dma(nw), dma(nn), dma(nx), dma(2, nz // 2), dma(nn), dma(2),
            dma(nx),
            pltpu.SemaphoreType.DMA((lanes, 2, 2, nz // 2)),
            dma(2, nz // 2),
            pltpu.SemaphoreType.DMA((2, 2, 2, max(nx // 2, 1))),
            dma(nn),
            dma(nw), dma(nn), dma(nw), dma(nz), dma(nx), dma(nn), dma(nz),
        ],
        compiler_params=pltpu.CompilerParams(
            collective_id=0, has_side_effects=True, vmem_limit_bytes=60 * 1024 * 1024
        ),
    )(panel, count, points, weight, basis, jacobi, agg, block, inverse)


def body(
    points, quad_weight, basis, jacobi, near_panel, near_count, near_block, agg_index, coarse_inverse, nz=NZ
):
    block_total, comps, point_count, rhs_count = basis.shape
    new_flat, hessenberg, upper = whole_step(
        near_panel,
        near_count,
        points,
        quad_weight[None, :],
        basis.reshape(block_total, comps * point_count, rhs_count),
        jacobi,
        agg_index,
        near_block,
        coarse_inverse,
        lax.axis_size("narrow"),
        lax.axis_size("wide"),
        nz,
    )
    return (new_flat.reshape(comps, point_count, rhs_count), hessenberg, upper)


def solution(mesh):
    in_specs = (
        P(None, ("narrow", "wide")),
        P(("narrow", "wide")),
        P(None, None, ("narrow", "wide"), None),
        P(None, ("narrow", "wide")),
        P(("narrow", "wide"), None),
        P(("narrow", "wide")),
        P(("narrow", "wide"), None, None, None),
        P(None, ("narrow", "wide")),
        P(None, "wide", "narrow"),
    )
    out_specs = (P(None, ("narrow", "wide"), None), P(), P())
    return jax.shard_map(body, mesh=mesh, in_specs=in_specs, out_specs=out_specs, check_vma=False)
```

```python
import functools

import jax
import jax.numpy as jnp
from jax import lax
from jax.experimental import pallas as pl
from jax.experimental.pallas import tpu as pltpu
from jax.sharding import PartitionSpec as P

NU = 0.3
DELTA2 = 1e-05
ELASTIC = 40.0
HIGH = lax.Precision.HIGHEST
MESH = pl.DeviceIdType.MESH
NZ = 8
PANEL = 16
HALF = 64


def mm(a, b, dims):
    return lax.dot_general(a, b, (dims, ((), ())), precision=HIGH, preferred_element_type=jnp.float32)


def swap(count, me, device, src, dst, sems, go):
    def one(k, carry):
        peer = lax.rem(me + k, count)
        copy = pltpu.make_async_remote_copy(
            src_ref=src(peer),
            dst_ref=dst,
            send_sem=sems.at[0, k],
            recv_sem=sems.at[1, k],
            device_id=device(peer),
            device_id_type=MESH,
        )
        if go:
            copy.start()
        else:
            copy.wait()
        return carry

    lax.fori_loop(1, count, one, 0)


def exchange(count, me, device, src, dst, sems):
    swap(count, me, device, src, dst, sems, True)
    swap(count, me, device, src, dst, sems, False)


def ring(count, me, device, block, half, sems, step, go):
    back = step - 1
    for way, peer, origin in ((0, me + 1, me + count - back), (1, me + count - 1, me + back)):
        peer, origin = lax.rem(peer, count), lax.rem(origin, count)
        ref = half(origin, way) if step == count // 2 else block(origin)
        copy = pltpu.make_async_remote_copy(
            src_ref=ref,
            dst_ref=ref,
            send_sem=sems.at[0, way, back],
            recv_sem=sems.at[1, way, back],
            device_id=device(peer),
            device_id_type=MESH,
        )
        if go:
            copy.start()
        else:
            copy.wait()


def slots_sum(ref, count):
    total = ref[0]
    for k in range(1, count):
        total = total + ref[k]
    return total


def greet(nn, nw, n, w, before, after):
    barrier = pltpu.get_barrier_semaphore()

    def wide_one(k, carry):
        pl.semaphore_signal(barrier, inc=1, device_id={"wide": lax.rem(w + k, nw)}, device_id_type=MESH)
        return carry

    def narrow_one(k, carry):
        pl.semaphore_signal(barrier, inc=1, device_id={"narrow": lax.rem(n + k, nn)}, device_id_type=MESH)
        return carry

    lax.fori_loop(1, nw, wide_one, 0)
    lax.fori_loop(1, nn, narrow_one, 0)
    for peer in (before, after):
        pl.semaphore_signal(barrier, inc=1, device_id=peer, device_id_type=MESH)
    return barrier


def factor(gram, work):
    size = gram.shape[0]
    rows = lax.broadcasted_iota(jnp.int32, (size, size), 0)
    cols = lax.broadcasted_iota(jnp.int32, (size, size), 1)
    work[:, 0:size] = gram
    work[:, size:] = (rows == cols).astype(jnp.float32)
    sub = lax.broadcasted_iota(jnp.int32, (PANEL, 1), 0)
    for base in range(0, size, PANEL):
        panel = work[base : base + PANEL, :]
        for k in range(PANEL):
            pivot = panel[k : k + 1, base + k : base + k + 1]
            row = panel[k : k + 1, :] * lax.rsqrt(pivot)
            left = panel[:, base + k : base + k + 1] * lax.rsqrt(pivot)
            panel = jnp.where(sub == k, row, jnp.where(sub > k, panel - left * row, panel))
        work[base : base + PANEL, :] = panel
        if base + PANEL < size:
            below = mm(panel[:, 0:size], panel, ((0,), (0,)))
            work[base + PANEL :, :] = work[base + PANEL :, :] - below[base + PANEL :, :]


def column(row, points):
    return jnp.transpose(jnp.broadcast_to(row, (points, points)))


def step_kernel(
    nn, nw, nz,
    panel_ref, count_ref, points_ref, weight_ref, basis_hbm, jacobi_ref, agg_ref, block_hbm, inverse_hbm,
    rest_ref, hess_ref, gram_ref,
    basis_ref, block_ref, inverse_ref,
    info, info_w, info_n, sources, columns, green,
    rhs_a, rhs_b, rhs_all, parts, part_slots, fields_a, fields_b, window, halo, far, far_slots, near,
    send_h, slots_h, mid_h, slots_n, full_h,
    send_g, slots_gz, mid_g, slots_gx, mid_g2, slots_gn, full_g,
    rest,
    sems_io, sems_iw, sems_in, sems_cn, sems_halo,
    sems_cax, sems_caz, sems_cbz, sems_cbx,
    sems_ax, sems_az, sems_bz, sems_bx, sems_far,
    sems_w, sems_n, sems_w2, sems_z, sems_x, sems_gn, sems_z2,
):
    f32, bf16 = jnp.float32, jnp.bfloat16
    n = lax.axis_index("narrow")
    w = lax.axis_index("wide")
    x, z = w // nz, lax.rem(w, nz)
    nx = nw // nz
    blocks, size = basis_ref.shape[0], basis_ref.shape[2]
    points = weight_ref.shape[1]
    coarse = inverse_ref.shape[1]
    flat = n * nw + w
    total = nn * nw

    def flat_peer(p):
        return {"narrow": p // nw, "wide": lax.rem(p, nw)}

    before, after = flat_peer(lax.rem(flat + total - 1, total)), flat_peer(lax.rem(flat + 1, total))
    barrier = greet(nn, nw, n, w, before, after)
    loads = [
        pltpu.make_async_copy(src, dst, sems_io.at[i])
        for i, (src, dst) in enumerate(((basis_hbm, basis_ref), (inverse_hbm, inverse_ref), (block_hbm, block_ref)))
    ]
    for load in loads:
        load.start()

    def wide_peer(p):
        return {"wide": p}

    def narrow_peer(p):
        return {"narrow": p}

    def z_peer(p):
        return {"wide": x * nz + p}

    def x_peer(p):
        return {"wide": p * nz + z}

    lanes = max(nx // 2, 1)

    def gathering(buf_a, buf_b, cut, sem_ax, sem_az, sem_bz, sem_bx):
        def a_first(go):
            swap(nx, x, x_peer, lambda p: buf_a.at[z, x], buf_a.at[z, x], sem_ax, go)

        def a_ring(j, step, go):
            ring(
                nz, z, z_peer,
                lambda p: buf_a.at[p, 2 * j : 2 * j + 2],
                lambda p, way: buf_a.at[p, 2 * j + way],
                sem_az.at[j], step, go,
            )

        def part(ref, way):
            return ref.at[:cut] if way == 0 else ref.at[cut:]

        def b_ring(step, go):
            ring(
                nz, z, z_peer,
                lambda p: buf_b.at[x, p],
                lambda p, way: part(buf_b.at[x, p], way),
                sem_bz, step, go,
            )

        def bx_ring(shift, step, go):
            for at, sign in ((2 * shift - 1, -1), (2 * shift, 1)):
                if at < 0 or at >= nz:
                    continue
                q = lax.rem(z + nz + sign * shift, nz)
                ring(
                    nx, x, x_peer,
                    lambda p: buf_b.at[p, q],
                    lambda p, way: part(buf_b.at[p, q], way),
                    sem_bx.at[at], step, go,
                )

        return a_first, a_ring, b_ring, bx_ring

    def run_gather(steps, opened, own, arrived, crossed):
        a_first, a_ring, b_ring, bx_ring = steps
        deep, wide_steps = nz // 2, nx // 2

        def next_b(step):
            b_ring(step, False)
            if step < deep:
                b_ring(step + 1, True)
            bx_ring(step, 1, True)

        def next_x(shift):
            bx_ring(shift, 1, False)
            if wide_steps > 1:
                bx_ring(shift, 2, True)

        a_first(True)
        b_ring(1, True)
        bx_ring(0, 1, True)
        opened()
        a_first(False)
        for j in range(lanes):
            a_ring(j, 1, True)
        next_b(1)
        next_x(0)
        own()
        for step in range(1, deep + 1):
            if step < deep:
                next_b(step + 1)
            next_x(step)
            for j in range(lanes):
                a_ring(j, step, False)
                if step < deep:
                    a_ring(j, step + 1, True)
            arrived(step)
        crossed(1)
        if wide_steps > 1:
            for shift in range(deep + 1):
                bx_ring(shift, 2, False)
            crossed(2)

    info[...] = jnp.zeros_like(info)
    info[0:2, :] = points_ref[...]
    info[2:3, :] = ELASTIC * weight_ref[...]
    info_n[n] = info[...]
    info_w[w] = info[...]

    ids = lax.broadcasted_iota(jnp.int32, (coarse, points), 0)
    member = [(ids == agg_ref[a : a + 1, :]).astype(f32) for a in range(2)]
    loads[0].wait()
    newest = [basis_ref[blocks - 1, a * points : (a + 1) * points, :] for a in range(2)]
    rhs = mm(member[0], newest[0], ((1,), (0,))) + mm(member[1], newest[1], ((1,), (0,)))
    rhs_a[z, x] = rhs[0 : coarse // 2, :]
    rhs_b[x, z] = rhs[coarse // 2 :, :]
    pl.semaphore_wait(barrier, nw + nn)
    swap(nn, n, narrow_peer, lambda p: info, info_n.at[n], sems_in, True)
    swap(nw, w, wide_peer, lambda p: info, info_w.at[w], sems_iw, True)
    chunks = nz + 2 * nx
    tall = 32
    pairs = nx // 2

    def prepare():
        swap(nn, n, narrow_peer, lambda p: info, info_n.at[n], sems_in, False)
        swap(nw, w, wide_peer, lambda p: info, info_w.at[w], sems_iw, False)
        lane = lax.broadcasted_iota(jnp.int32, (8, points), 1)
        for p in range(nz):
            for m in range(pairs):
                one, two = info_w[(2 * m) * nz + p], info_w[(2 * m + 1) * nz + p]
                sources[p, m] = jnp.where(lane < HALF, one, pltpu.roll(two, HALF, 1))
        for p in range(nx):
            for h in range(2):
                for m in range(pairs):
                    at = p * nz + h * (nz // 2) + 2 * m
                    one, two = info_w[at], info_w[at + 1]
                    sources[nz + 2 * p + h, m] = jnp.where(lane < HALF, pltpu.roll(one, HALF, 1), two)
        for t in range(nn):
            tile = info_n[t]
            for a in range(2):
                columns[t, a] = column(tile[a : a + 1, :], points)

    def evaluate(first, last):
        def unit(i, carry):
            c, t = i // nn, lax.rem(i, nn)
            for m in range(pairs):
                src = sources[c, m]
                sx, sy, sw = src[0:1, :], src[1:2, :], src[2:3, :]
                for r in range(0, points, tall):
                    dx = columns[t, 0, r : r + tall, :] - sx
                    dy = columns[t, 1, r : r + tall, :] - sy
                    xx, yy = dx * dx, dy * dy
                    square = xx + yy + DELTA2
                    inv = 1.0 / square
                    log_part = (-0.5 * (3.0 - 4.0 * NU)) * jnp.log(square)
                    rows = pl.ds(pl.multiple_of(t * points + r, tall), tall)
                    cols = slice(m * points, (m + 1) * points)
                    green[c, 0, rows, cols] = (sw * (log_part + xx * inv)).astype(bf16)
                    green[c, 1, rows, cols] = (sw * (dx * dy * inv)).astype(bf16)
                    green[c, 2, rows, cols] = (sw * (log_part + yy * inv)).astype(bf16)
            return carry

        lax.fori_loop(first, last, unit, 0)

    done = [0]

    def fill(share):
        last = min(done[0] + share * chunks * nn // 128, chunks * nn)
        evaluate(done[0], last)
        done[0] = last

    run_gather(
        gathering(rhs_a, rhs_b, 16, sems_cax, sems_caz, sems_cbz, sems_cbx),
        lambda: None, prepare, lambda step: fill(16), lambda step: None,
    )
    for p in range(nx):
        for q in range(nz):
            rhs_all[p, q, 0 : coarse // 2, :] = rhs_a[q, p]
            rhs_all[p, q, coarse // 2 :, :] = rhs_b[p, q]
    loads[1].wait()

    inverse = inverse_ref[...].reshape(nn * coarse, nw * coarse)
    parts[...] = mm(inverse, rhs_all[...].reshape(nw * coarse, size), ((1,), (0,))).reshape(nn, coarse, size)
    swap(nn, n, narrow_peer, lambda p: parts.at[p], part_slots.at[n], sems_cn, True)
    part_slots[n] = parts[n]
    fill(32)
    swap(nn, n, narrow_peer, lambda p: parts.at[p], part_slots.at[n], sems_cn, False)
    sol = slots_sum(part_slots, nn)
    for a in range(2):
        lifted = mm(member[a], sol, ((0,), (0,)))
        field = (column(jacobi_ref[a : a + 1, :], points) * newest[a] + lifted).astype(bf16)
        window[HALF : HALF + points, a * size : (a + 1) * size] = field
    fields_a[z, x] = window[HALF : 2 * HALF, :]
    fields_b[x, z] = window[2 * HALF : 3 * HALF, :]

    def halo_copy(way, src, peer, go):
        copy = pltpu.make_async_remote_copy(
            src_ref=src, dst_ref=halo.at[way], send_sem=sems_halo.at[0, way], recv_sem=sems_halo.at[1, way],
            device_id=peer, device_id_type=MESH,
        )
        if go:
            copy.start()
        else:
            copy.wait()

    def halos(go):
        halo_copy(0, fields_b.at[x, z], after, go)
        halo_copy(1, fields_a.at[z, x], before, go)

    def accumulate(c, field, first):
        left, right = field[:, 0:size], field[:, size:]

        def rows_of(i, carry):
            rows = pl.ds(pl.multiple_of(i * 2 * points, 2 * points), 2 * points)
            cross = jnp.dot(green[c, 1, rows, :], field, preferred_element_type=f32)
            one = jnp.dot(green[c, 0, rows, :], left, preferred_element_type=f32) + cross[:, size:]
            two = jnp.dot(green[c, 2, rows, :], right, preferred_element_type=f32) + cross[:, 0:size]
            if first:
                far[rows, 0:size] = one
                far[rows, size:] = two
            else:
                far[rows, 0:size] = far[rows, 0:size] + one
                far[rows, size:] = far[rows, size:] + two
            return carry

        lax.fori_loop(0, nn // 2, rows_of, 0)

    def take_a(p, first=False):
        p = lax.rem(p, nz)
        accumulate(p, fields_a[p].reshape(nx * HALF, 2 * size), first)

    def take_b(p):
        p = lax.rem(p, nx)
        for h in range(2):
            part = fields_b[p, h * (nz // 2) : (h + 1) * (nz // 2)]
            accumulate(nz + 2 * p + h, part.reshape(nz // 2 * HALF, 2 * size), False)

    def near_field():
        halos(False)
        loads[2].wait()
        window[0:HALF, :] = halo[0]
        window[HALF + points :, :] = halo[1]
        q = block_ref.shape[2] // 2
        panels, slots = block_ref.shape[0], block_ref.shape[1]

        reach = points + 2 * HALF
        row_id = lax.broadcasted_iota(jnp.int32, (q, reach), 0)
        col_id = lax.broadcasted_iota(jnp.int32, (q, reach), 1)

        def one_panel(p, carry):
            live = jnp.full((q, reach), count_ref[p], jnp.int32)
            picks = []
            for k in range(slots):
                start = jnp.full((q, reach), (panel_ref[p, k] - flat * panels) * q + HALF, jnp.int32)
                picks.append(((col_id == start + row_id) & (live > k)).astype(f32))
            pick = jnp.concatenate(picks, axis=0).astype(bf16)
            rows = jnp.dot(pick, window[...], preferred_element_type=f32).astype(bf16)
            total = jnp.zeros((2 * q, size), f32)
            for k in range(slots):
                one = rows[k * q : (k + 1) * q, :]
                both = jnp.concatenate([one[:, 0:size], one[:, size:]], axis=0)
                total = total + jnp.dot(block_ref[p, k], both, preferred_element_type=f32)
            for a in range(2):
                near[pl.ds(pl.multiple_of(a * points + p * q, q), q), :] = total[a * q : (a + 1) * q, :]
            return carry

        lax.fori_loop(0, panels, one_panel, 0)

    def opened():
        halos(True)
        fill(16)

    def arrived(step):
        take_a(z + nz - step)
        if step < nz // 2:
            take_a(z + step)
        if step == 1:
            near_field()
        fill(16)

    def crossed(step):
        if step == 1:
            fill(chunks * nn)
            take_b(x)
        take_b(x + nx - step)
        if step < nx // 2:
            take_b(x + step)

    run_gather(
        gathering(fields_a, fields_b, HALF // 2, sems_ax, sems_az, sems_bz, sems_bx),
        opened, lambda: take_a(z, True), arrived, crossed,
    )

    def target(p):
        return far.at[pl.ds(pl.multiple_of(p * points, points), points), :]

    swap(nn, n, narrow_peer, target, far_slots.at[n], sems_far, True)
    far_slots[n] = far[pl.ds(pl.multiple_of(n * points, points), points), :]
    swap(nn, n, narrow_peer, target, far_slots.at[n], sems_far, False)
    far_sum = slots_sum(far_slots, nn)
    image = jnp.concatenate(
        [
            0.5 * window[HALF : HALF + points, a * size : (a + 1) * size].astype(f32)
            + far_sum[:, a * size : (a + 1) * size]
            + near[a * points : (a + 1) * points, :]
            for a in range(2)
        ],
        axis=0,
    )

    spread = column(weight_ref[...], points)
    scale = jnp.concatenate([spread, spread], axis=0)
    weighted = image * scale
    for j in range(blocks):
        send_h[j * size : (j + 1) * size, :] = mm(basis_ref[j], weighted, ((0,), (0,)))
    step = blocks * size // nw

    def chunk(ref, p, rows):
        return ref.at[pl.ds(pl.multiple_of(p * rows, rows), rows), :]

    swap(nw, w, wide_peer, lambda p: chunk(send_h, p, step), slots_h.at[w], sems_w, True)
    slots_h[w] = send_h[pl.ds(pl.multiple_of(w * step, step), step), :]
    swap(nw, w, wide_peer, lambda p: chunk(send_h, p, step), slots_h.at[w], sems_w, False)
    mid_h[...] = slots_sum(slots_h, nw)
    swap(nn, n, narrow_peer, lambda p: mid_h, slots_n.at[n], sems_n, True)
    slots_n[n] = mid_h[...]
    swap(nn, n, narrow_peer, lambda p: mid_h, slots_n.at[n], sems_n, False)
    full_h[pl.ds(pl.multiple_of(w * step, step), step), :] = slots_sum(slots_n, nn)
    exchange(nw, w, wide_peer, lambda p: chunk(full_h, w, step), chunk(full_h, w, step), sems_w2)
    out_h = pltpu.make_async_copy(full_h, hess_ref, sems_io.at[3])
    out_h.start()
    remainder = image
    for j in range(blocks):
        part = full_h[j * size : (j + 1) * size, :]
        remainder = remainder - mm(basis_ref[j], part, ((1,), (0,)))
    rest[...] = remainder
    out_rest = pltpu.make_async_copy(rest, rest_ref, sems_io.at[4])
    out_rest.start()
    send_g[...] = mm(remainder * scale, remainder, ((0,), (0,)))
    gstep = size // nz
    swap(nz, z, z_peer, lambda p: chunk(send_g, p, gstep), slots_gz.at[z], sems_z, True)
    slots_gz[z] = send_g[pl.ds(pl.multiple_of(z * gstep, gstep), gstep), :]
    swap(nz, z, z_peer, lambda p: chunk(send_g, p, gstep), slots_gz.at[z], sems_z, False)
    mid_g[...] = slots_sum(slots_gz, nz)
    swap(nx, x, x_peer, lambda p: mid_g, slots_gx.at[x], sems_x, True)
    slots_gx[x] = mid_g[...]
    swap(nx, x, x_peer, lambda p: mid_g, slots_gx.at[x], sems_x, False)
    mid_g2[...] = slots_sum(slots_gx, nx)
    swap(nn, n, narrow_peer, lambda p: mid_g2, slots_gn.at[n], sems_gn, True)
    slots_gn[n] = mid_g2[...]
    swap(nn, n, narrow_peer, lambda p: mid_g2, slots_gn.at[n], sems_gn, False)
    full_g[pl.ds(pl.multiple_of(z * gstep, gstep), gstep), :] = slots_sum(slots_gn, nn)
    exchange(nz, z, z_peer, lambda p: chunk(full_g, z, gstep), chunk(full_g, z, gstep), sems_z2)
    gram_ref[...] = full_g[...]
    out_h.wait()
    out_rest.wait()


def whole_step(panel, count, points, weight, basis, jacobi, agg, block, inverse, nn, nw, nz):
    blocks, rows, size = basis.shape
    f32, bf16 = jnp.float32, jnp.bfloat16
    pts = weight.shape[1]
    coarse = inverse.shape[1]
    vmem = pl.BlockSpec(memory_space=pltpu.VMEM)
    smem = pl.BlockSpec(memory_space=pltpu.SMEM)
    hbm = pl.BlockSpec(memory_space=pl.ANY)
    step, gstep, nx = blocks * size // nw, size // nz, nw // nz
    chunks, cols = nz + 2 * nx, nx * HALF
    dma = lambda *c: pltpu.SemaphoreType.DMA((2, *c))
    lanes = max(nx // 2, 1)
    buf = pltpu.VMEM
    gather_sems = (
        dma(nx),
        pltpu.SemaphoreType.DMA((lanes, 2, 2, nz // 2)),
        dma(2, nz // 2),
        pltpu.SemaphoreType.DMA((nz, 2, 2, nx // 2)),
    )
    return pl.pallas_call(
        functools.partial(step_kernel, nn, nw, nz),
        name="step",
        out_shape=(
            jax.ShapeDtypeStruct((rows, size), f32),
            jax.ShapeDtypeStruct((blocks * size, size), f32),
            jax.ShapeDtypeStruct((size, size), f32),
        ),
        in_specs=[smem] * 2 + [vmem] * 2 + [hbm] + [vmem] * 2 + [hbm] * 2,
        out_specs=(hbm, hbm, vmem),
        scratch_shapes=[
            buf(basis.shape, f32),
            buf(block.shape, bf16),
            buf(inverse.shape, f32),
            buf((8, pts), f32),
            buf((nw, 8, pts), f32),
            buf((nn, 8, pts), f32),
            buf((chunks, nx // 2, 8, pts), f32),
            buf((nn, 2, pts, pts), f32),
            buf((chunks, 3, nn * pts, cols), bf16),
            buf((nz, nx, coarse // 2, size), f32),
            buf((nx, nz, coarse // 2, size), f32),
            buf((nx, nz, coarse, size), f32),
            buf((nn, coarse, size), f32),
            buf((nn, coarse, size), f32),
            buf((nz, nx, HALF, 2 * size), bf16),
            buf((nx, nz, HALF, 2 * size), bf16),
            buf((pts + 2 * HALF, 2 * size), bf16),
            buf((2, HALF, 2 * size), bf16),
            buf((nn * pts, 2 * size), f32),
            buf((nn, pts, 2 * size), f32),
            buf((rows, size), f32),
            buf((blocks * size, size), f32),
            buf((nw, step, size), f32),
            buf((step, size), f32),
            buf((nn, step, size), f32),
            buf((blocks * size, size), f32),
            buf((size, size), f32),
            buf((nz, gstep, size), f32),
            buf((gstep, size), f32),
            buf((nx, gstep, size), f32),
            buf((gstep, size), f32),
            buf((nn, gstep, size), f32),
            buf((size, size), f32),
            buf((rows, size), f32),
            pltpu.SemaphoreType.DMA((5,)),
            dma(nw), dma(nn), dma(nn), dma(2),
            *gather_sems, *gather_sems,
            dma(nn),
            dma(nw), dma(nn), dma(nw), dma(nz), dma(nx), dma(nn), dma(nz),
        ],
        compiler_params=pltpu.CompilerParams(
            collective_id=0, has_side_effects=True, vmem_limit_bytes=60 * 1024 * 1024
        ),
    )(panel, count, points, weight, basis, jacobi, agg, block, inverse)


def finish_kernel(gram_ref, rest_hbm, hess_hbm, new_ref, hess_out, upper_ref, rest, hess, work, sems):
    size = gram_ref.shape[0]
    get_rest = pltpu.make_async_copy(rest_hbm, rest, sems.at[0])
    get_hess = pltpu.make_async_copy(hess_hbm, hess, sems.at[1])
    put_hess = pltpu.make_async_copy(hess, hess_out, sems.at[2])
    get_rest.start()
    get_hess.start()
    get_hess.wait()
    put_hess.start()
    factor(gram_ref[...], work)
    row = lax.broadcasted_iota(jnp.int32, (size, size), 0)
    col = lax.broadcasted_iota(jnp.int32, (size, size), 1)
    upper_ref[...] = jnp.where(row <= col, work[:, 0:size], 0.0)
    get_rest.wait()
    new_ref[...] = mm(rest[...], work[:, size:], ((1,), (1,)))
    put_hess.wait()


def finish(gram, rest, hess):
    f32 = jnp.float32
    size = gram.shape[0]
    vmem = pl.BlockSpec(memory_space=pltpu.VMEM)
    hbm = pl.BlockSpec(memory_space=pl.ANY)
    return pl.pallas_call(
        finish_kernel,
        name="finish",
        out_shape=(
            jax.ShapeDtypeStruct(rest.shape, f32),
            jax.ShapeDtypeStruct(hess.shape, f32),
            jax.ShapeDtypeStruct(gram.shape, f32),
        ),
        in_specs=[vmem, hbm, hbm],
        out_specs=(vmem, hbm, vmem),
        scratch_shapes=[
            pltpu.VMEM(rest.shape, f32),
            pltpu.VMEM(hess.shape, f32),
            pltpu.VMEM((size, 2 * size), f32),
            pltpu.SemaphoreType.DMA((3,)),
        ],
    )(gram, rest, hess)


def body(
    points, quad_weight, basis, jacobi, near_panel, near_count, near_block, agg_index, coarse_inverse, nz=NZ
):
    block_total, comps, point_count, rhs_count = basis.shape
    rest, hess, gram = whole_step(
        near_panel,
        near_count,
        points,
        quad_weight[None, :],
        basis.reshape(block_total, comps * point_count, rhs_count),
        jacobi,
        agg_index,
        near_block,
        coarse_inverse,
        lax.axis_size("narrow"),
        lax.axis_size("wide"),
        nz,
    )
    new_flat, hess, upper = finish(gram, rest, hess)
    return (
        new_flat.reshape(comps, point_count, rhs_count),
        hess.reshape(block_total, rhs_count, rhs_count),
        upper,
    )


def solution(mesh):
    in_specs = (
        P(None, ("narrow", "wide")),
        P(("narrow", "wide")),
        P(None, None, ("narrow", "wide"), None),
        P(None, ("narrow", "wide")),
        P(("narrow", "wide"), None),
        P(("narrow", "wide")),
        P(("narrow", "wide"), None, None, None),
        P(None, ("narrow", "wide")),
        P(None, "wide", "narrow"),
    )
    out_specs = (P(None, ("narrow", "wide"), None), P(), P())
    return jax.shard_map(body, mesh=mesh, in_specs=in_specs, out_specs=out_specs, check_vma=False)
```

```python
import functools

import jax
import jax.numpy as jnp
from jax import lax
from jax.experimental import pallas as pl
from jax.experimental.pallas import tpu as pltpu
from jax.sharding import PartitionSpec as P

NU = 0.3
DELTA2 = 1e-05
ELASTIC = 40.0
HIGH = lax.Precision.HIGHEST
MESH = pl.DeviceIdType.MESH
NZ = 8
PANEL = 32
GROUP = 8
HALF = 64


def mm(a, b, dims):
    return lax.dot_general(a, b, (dims, ((), ())), precision=HIGH, preferred_element_type=jnp.float32)


def drain(sem, ref):
    pltpu.make_async_copy(ref, ref, sem).wait()


def swap(count, me, device, src, dst, sems, whole, go):
    if not go:
        drain(sems.at[0], whole)
        drain(sems.at[1], whole)
        return

    def one(k, carry):
        peer = lax.rem(me + k, count)
        pltpu.make_async_remote_copy(
            src_ref=src(peer),
            dst_ref=dst,
            send_sem=sems.at[0],
            recv_sem=sems.at[1],
            device_id=device(peer),
            device_id_type=MESH,
        ).start()
        return carry

    lax.fori_loop(1, count, one, 0)


def exchange(count, me, device, src, dst, sems, whole):
    swap(count, me, device, src, dst, sems, whole, True)
    swap(count, me, device, src, dst, sems, whole, False)


def ring(count, me, device, block, half, send_sem, recv_sem, step):
    back = step - 1
    for way, peer, origin in ((0, me + 1, me + count - back), (1, me + count - 1, me + back)):
        peer, origin = lax.rem(peer, count), lax.rem(origin, count)
        ref = half(origin, way) if step == count // 2 else block(origin)
        pltpu.make_async_remote_copy(
            src_ref=ref,
            dst_ref=ref,
            send_sem=send_sem,
            recv_sem=recv_sem,
            device_id=device(peer),
            device_id_type=MESH,
        ).start()


def slots_sum(ref, count):
    total = ref[0]
    for k in range(1, count):
        total = total + ref[k]
    return total


def greet(groups, others):
    barrier = pltpu.get_barrier_semaphore()
    for count, me, device in groups:

        def one(k, carry):
            pl.semaphore_signal(barrier, inc=1, device_id=device(lax.rem(me + k, count)), device_id_type=MESH)
            return carry

        lax.fori_loop(1, count, one, 0)
    for peer in others:
        pl.semaphore_signal(barrier, inc=1, device_id=peer, device_id_type=MESH)
    return barrier, sum(count - 1 for count, _, _ in groups) + len(others)


def factor(gram, work):
    size = gram.shape[0]
    rows = lax.broadcasted_iota(jnp.int32, (size, size), 0)
    cols = lax.broadcasted_iota(jnp.int32, (size, size), 1)
    work[:, 0:size] = gram
    work[:, size:] = (rows == cols).astype(jnp.float32)
    sub = lax.broadcasted_iota(jnp.int32, (PANEL, size), 0)
    for base in range(0, size, PANEL):
        sides = [work[base : base + PANEL, 0:size], work[base : base + PANEL, size:]]
        for k in range(0, PANEL, GROUP):
            lefts = [
                jnp.broadcast_to(sides[0][:, base + k + j : base + k + j + 1], (PANEL, size)) for j in range(GROUP)
            ]
            tops = [[side[k + j : k + j + 1, :] for side in sides] for j in range(GROUP)]
            for j in range(GROUP):
                inv = lax.rsqrt(lefts[j][k + j : k + j + 1, :])
                lefts[j] = lefts[j] * inv
                tops[j] = [top * inv for top in tops[j]]
                for i in range(j + 1, GROUP):
                    share = lefts[j][k + i : k + i + 1, :]
                    lefts[i] = lefts[i] - lefts[j] * share
                    tops[i] = [top - share * done for top, done in zip(tops[i], tops[j])]
            for s in range(2):
                new = sides[s]
                for j in range(GROUP):
                    new = new - lefts[j] * tops[j][s]
                new = jnp.where(sub >= k + GROUP, new, sides[s])
                for j in range(GROUP):
                    new = jnp.where(sub == k + j, tops[j][s], new)
                sides[s] = new
        work[base : base + PANEL, 0:size] = sides[0]
        work[base : base + PANEL, size:] = sides[1]
        if base + PANEL < size:
            panel = jnp.concatenate(sides, axis=1)
            below = mm(sides[0], panel, ((0,), (0,)))
            work[base + PANEL :, :] = work[base + PANEL :, :] - below[base + PANEL :, :]


def column(row, points):
    return jnp.transpose(jnp.broadcast_to(row, (points, points)))


def step_kernel(
    nn, nw, nz,
    panel_ref, count_ref, points_ref, weight_ref, basis_hbm, jacobi_ref, agg_ref, block_hbm, inverse_hbm,
    rest_ref, hess_ref, gram_ref,
    basis_ref, block_ref, inverse_ref,
    info, info_w, info_n, sources, columns, green,
    rhs_a, rhs_b, rhs_all, parts, part_slots, fields_a, fields_b, window, halo, far, far_slots, near,
    send_h, slots_z, mid_z, slots_x, mid_h, slots_n, full_h,
    send_g, slots_gz, mid_g, slots_gx, mid_g2, slots_gn, full_g,
    rest,
    sems_io, sems_ix, sems_iz, sems_in, sems_cn, sems_halo,
    sems_cax, sems_cs, sems_caz, sems_cbz, sems_cbx,
    sems_ax, sems_as, sems_az, sems_bz, sems_bx, sems_far,
    sems_hz, sems_hx, sems_n, sems_hx2, sems_hz2, sems_z, sems_x, sems_gn, sems_z2,
):
    f32, bf16 = jnp.float32, jnp.bfloat16
    n = lax.axis_index("narrow")
    w = lax.axis_index("wide")
    x, z = w // nz, lax.rem(w, nz)
    nx = nw // nz
    blocks, size = basis_ref.shape[0], basis_ref.shape[2]
    points = weight_ref.shape[1]
    coarse = inverse_ref.shape[1]
    flat = n * nw + w
    total = nn * nw

    def flat_peer(p):
        return {"narrow": p // nw, "wide": lax.rem(p, nw)}

    before, after = flat_peer(lax.rem(flat + total - 1, total)), flat_peer(lax.rem(flat + 1, total))
    def narrow_peer(p):
        return {"narrow": p}

    def z_peer(p):
        return {"wide": x * nz + p}

    def x_peer(p):
        return {"wide": p * nz + z}

    barrier, greeted = greet(((nn, n, narrow_peer), (nx, x, x_peer), (nz, z, z_peer)), (before, after))
    loads = [
        pltpu.make_async_copy(src, dst, sems_io.at[i])
        for i, (src, dst) in enumerate(((basis_hbm, basis_ref), (inverse_hbm, inverse_ref), (block_hbm, block_ref)))
    ]
    for load in loads:
        load.start()

    lanes = max(nx // 2, 1)

    def gathering(buf_a, buf_b, cut, sem_ax, sem_send, sem_az, sem_bz, sem_bx):
        deep, cross = nz // 2, nx // 2

        def a_first(go):
            swap(nx, x, x_peer, lambda p: buf_a.at[z, x], buf_a.at[z, x], sem_ax, buf_a.at[0, 0 : nx - 1], go)

        def a_ring(j, step, go):
            if not go:
                drain(sem_az.at[j, step - 1], buf_a.at[0:2, 0:2] if step < deep else buf_a.at[0, 0:2])
                return
            ring(
                nz, z, z_peer,
                lambda p: buf_a.at[p, 2 * j : 2 * j + 2],
                lambda p, way: buf_a.at[p, 2 * j + way],
                sem_send.at[0], sem_az.at[j, step - 1], step,
            )

        def part(ref, way):
            return ref.at[:cut] if way == 0 else ref.at[cut:]

        def b_ring(step, go):
            if not go:
                drain(sem_bz.at[step - 1], buf_b.at[0, 0:2] if step < deep else buf_b.at[0, 0])
                return
            ring(
                nz, z, z_peer,
                lambda p: buf_b.at[x, p],
                lambda p, way: part(buf_b.at[x, p], way),
                sem_send.at[1], sem_bz.at[step - 1], step,
            )

        def bx_ring(shift, step, go):
            signs = [sign for at, sign in ((2 * shift - 1, -1), (2 * shift, 1)) if 0 <= at < nz]
            if not go:
                drain(sem_bx.at[shift], buf_b.at[0, 0 : len(signs) * (2 if step < cross else 1)])
                return
            for sign in signs:
                q = lax.rem(z + nz + sign * shift, nz)
                ring(
                    nx, x, x_peer,
                    lambda p: buf_b.at[p, q],
                    lambda p, way: part(buf_b.at[p, q], way),
                    sem_send.at[2], sem_bx.at[shift if step == 1 else deep + 1], step,
                )

        def close():
            if cross > 1:
                drain(sem_bx.at[deep + 1], buf_b.at[0])
            drain(sem_send.at[0], buf_a.at[0 : nz - 1])
            drain(sem_send.at[1], buf_b.at[0, 0 : nz - 1])
            drain(sem_send.at[2], buf_b.at[0 : nx - 1])

        return a_first, a_ring, b_ring, bx_ring, close

    def run_gather(steps, opened, own, arrived, crossed):
        a_first, a_ring, b_ring, bx_ring, close = steps
        deep, wide_steps = nz // 2, nx // 2

        def next_b(step):
            b_ring(step, False)
            if step < deep:
                b_ring(step + 1, True)
            bx_ring(step, 1, True)

        def next_x(shift):
            bx_ring(shift, 1, False)
            if wide_steps > 1:
                bx_ring(shift, 2, True)

        a_first(True)
        b_ring(1, True)
        bx_ring(0, 1, True)
        opened()
        a_first(False)
        for j in range(lanes):
            a_ring(j, 1, True)
        next_b(1)
        next_x(0)
        own()
        for step in range(1, deep + 1):
            if step < deep:
                next_b(step + 1)
            next_x(step)
            if step == deep:
                crossed(1)
            for j in range(lanes):
                a_ring(j, step, False)
                if step < deep:
                    a_ring(j, step + 1, True)
            arrived(step)
        close()
        if wide_steps > 1:
            crossed(2)

    info[...] = jnp.zeros_like(info)
    info[0:2, :] = points_ref[...]
    info[2:3, :] = ELASTIC * weight_ref[...]
    info_n[n] = info[...]
    info_w[z, x] = info[...]

    ids = lax.broadcasted_iota(jnp.int32, (coarse, points), 0)
    member = [(ids == agg_ref[a : a + 1, :]).astype(f32) for a in range(2)]
    loads[0].wait()
    newest = [basis_ref[blocks - 1, a * points : (a + 1) * points, :] for a in range(2)]
    rhs = mm(member[0], newest[0], ((1,), (0,))) + mm(member[1], newest[1], ((1,), (0,)))
    rhs_a[z, x] = rhs[0 : coarse // 2, :]
    rhs_b[x, z] = rhs[coarse // 2 :, :]
    pl.semaphore_wait(barrier, greeted)
    swap(nx, x, x_peer, lambda p: info, info_w.at[z, x], sems_ix, info_w.at[0, 0 : nx - 1], True)
    swap(nn, n, narrow_peer, lambda p: info, info_n.at[n], sems_in, info_n.at[0 : nn - 1], True)
    chunks = nz + 2 * nx
    tall = 32
    pairs = nx // 2

    def spread_info():
        swap(nx, x, x_peer, lambda p: info, info_w.at[z, x], sems_ix, info_w.at[0, 0 : nx - 1], False)
        swap(nz, z, z_peer, lambda p: info_w.at[z], info_w.at[z], sems_iz, info_w.at[0 : nz - 1], True)

    def prepare():
        swap(nn, n, narrow_peer, lambda p: info, info_n.at[n], sems_in, info_n.at[0 : nn - 1], False)
        swap(nz, z, z_peer, lambda p: info_w.at[z], info_w.at[z], sems_iz, info_w.at[0 : nz - 1], False)
        lane = lax.broadcasted_iota(jnp.int32, (8, points), 1)
        for p in range(nz):
            for m in range(pairs):
                one, two = info_w[p, 2 * m], info_w[p, 2 * m + 1]
                sources[p, m] = jnp.where(lane < HALF, one, pltpu.roll(two, HALF, 1))
        for p in range(nx):
            for h in range(2):
                for m in range(pairs):
                    at = h * (nz // 2) + 2 * m
                    one, two = info_w[at, p], info_w[at + 1, p]
                    sources[nz + 2 * p + h, m] = jnp.where(lane < HALF, pltpu.roll(one, HALF, 1), two)
        for t in range(nn):
            tile = info_n[t]
            for a in range(2):
                columns[t, a] = column(tile[a : a + 1, :], points)

    def evaluate(first, last):
        def unit(i, carry):
            c, t = i // nn, lax.rem(i, nn)
            for m in range(pairs):
                src = sources[c, m]
                sx, sy, sw = src[0:1, :], src[1:2, :], src[2:3, :]
                for r in range(0, points, tall):
                    dx = columns[t, 0, r : r + tall, :] - sx
                    dy = columns[t, 1, r : r + tall, :] - sy
                    xx, yy = dx * dx, dy * dy
                    square = xx + yy + DELTA2
                    inv = 1.0 / square
                    log_part = (-0.5 * (3.0 - 4.0 * NU)) * jnp.log(square)
                    rows = pl.ds(pl.multiple_of(t * points + r, tall), tall)
                    cols = slice(m * points, (m + 1) * points)
                    green[c, 0, rows, cols] = (sw * (log_part + xx * inv)).astype(bf16)
                    green[c, 1, rows, cols] = (sw * (dx * dy * inv)).astype(bf16)
                    green[c, 2, rows, cols] = (sw * (log_part + yy * inv)).astype(bf16)
            return carry

        lax.fori_loop(first, last, unit, 0)

    done = [0]

    def fill(share):
        last = min(done[0] + share * chunks * nn // 128, chunks * nn)
        evaluate(done[0], last)
        done[0] = last

    run_gather(
        gathering(rhs_a, rhs_b, 16, sems_cax, sems_cs, sems_caz, sems_cbz, sems_cbx),
        spread_info, prepare, lambda step: fill(16), lambda step: None,
    )
    for p in range(nx):
        for q in range(nz):
            rhs_all[p, q, 0 : coarse // 2, :] = rhs_a[q, p]
            rhs_all[p, q, coarse // 2 :, :] = rhs_b[p, q]
    loads[1].wait()

    inverse = inverse_ref[...].reshape(nn * coarse, nw * coarse)
    parts[...] = mm(inverse, rhs_all[...].reshape(nw * coarse, size), ((1,), (0,))).reshape(nn, coarse, size)
    swap(nn, n, narrow_peer, lambda p: parts.at[p], part_slots.at[n], sems_cn, part_slots.at[0 : nn - 1], True)
    part_slots[n] = parts[n]
    fill(32)
    swap(nn, n, narrow_peer, lambda p: parts.at[p], part_slots.at[n], sems_cn, part_slots.at[0 : nn - 1], False)
    sol = slots_sum(part_slots, nn)
    for a in range(2):
        lifted = mm(member[a], sol, ((0,), (0,)))
        field = (column(jacobi_ref[a : a + 1, :], points) * newest[a] + lifted).astype(bf16)
        window[HALF : HALF + points, a * size : (a + 1) * size] = field
    fields_a[z, x] = window[HALF : 2 * HALF, :]
    fields_b[x, z] = window[2 * HALF : 3 * HALF, :]

    def halo_copy(way, src, peer, go):
        copy = pltpu.make_async_remote_copy(
            src_ref=src, dst_ref=halo.at[way], send_sem=sems_halo.at[0, way], recv_sem=sems_halo.at[1, way],
            device_id=peer, device_id_type=MESH,
        )
        if go:
            copy.start()
        else:
            copy.wait()

    def halos(go):
        halo_copy(0, fields_b.at[x, z], after, go)
        halo_copy(1, fields_a.at[z, x], before, go)

    def accumulate(c, field, first):
        left, right = field[:, 0:size], field[:, size:]

        def rows_of(i, carry):
            rows = pl.ds(pl.multiple_of(i * 2 * points, 2 * points), 2 * points)
            cross = jnp.dot(green[c, 1, rows, :], field, preferred_element_type=f32)
            one = jnp.dot(green[c, 0, rows, :], left, preferred_element_type=f32) + cross[:, size:]
            two = jnp.dot(green[c, 2, rows, :], right, preferred_element_type=f32) + cross[:, 0:size]
            if first:
                far[rows, 0:size] = one
                far[rows, size:] = two
            else:
                far[rows, 0:size] = far[rows, 0:size] + one
                far[rows, size:] = far[rows, size:] + two
            return carry

        lax.fori_loop(0, nn // 2, rows_of, 0)

    def take_a(p, first=False):
        p = lax.rem(p, nz)
        accumulate(p, fields_a[p].reshape(nx * HALF, 2 * size), first)

    def take_b(p):
        p = lax.rem(p, nx)
        for h in range(2):
            part = fields_b[p, h * (nz // 2) : (h + 1) * (nz // 2)]
            accumulate(nz + 2 * p + h, part.reshape(nz // 2 * HALF, 2 * size), False)

    def near_field():
        halos(False)
        loads[2].wait()
        window[0:HALF, :] = halo[0]
        window[HALF + points :, :] = halo[1]
        q = block_ref.shape[2] // 2
        panels, slots = block_ref.shape[0], block_ref.shape[1]

        reach = points + 2 * HALF
        row_id = lax.broadcasted_iota(jnp.int32, (q, reach), 0)
        col_id = lax.broadcasted_iota(jnp.int32, (q, reach), 1)

        def one_panel(p, carry):
            live = jnp.full((q, reach), count_ref[p], jnp.int32)
            picks = []
            for k in range(slots):
                start = jnp.full((q, reach), (panel_ref[p, k] - flat * panels) * q + HALF, jnp.int32)
                picks.append(((col_id == start + row_id) & (live > k)).astype(f32))
            pick = jnp.concatenate(picks, axis=0).astype(bf16)
            rows = jnp.dot(pick, window[...], preferred_element_type=f32).astype(bf16)
            total = jnp.zeros((2 * q, size), f32)
            for k in range(slots):
                one = rows[k * q : (k + 1) * q, :]
                both = jnp.concatenate([one[:, 0:size], one[:, size:]], axis=0)
                total = total + jnp.dot(block_ref[p, k], both, preferred_element_type=f32)
            for a in range(2):
                near[pl.ds(pl.multiple_of(a * points + p * q, q), q), :] = total[a * q : (a + 1) * q, :]
            return carry

        lax.fori_loop(0, panels, one_panel, 0)

    def opened():
        halos(True)
        fill(16)

    def arrived(step):
        take_a(z + nz - step)
        if step < nz // 2:
            take_a(z + step)
        if step == 1:
            near_field()
        fill(16)

    def crossed(step):
        if step == 1:
            fill(128)
            take_b(x)
        take_b(x + nx - step)
        if step < nx // 2:
            take_b(x + step)

    run_gather(
        gathering(fields_a, fields_b, HALF // 2, sems_ax, sems_as, sems_az, sems_bz, sems_bx),
        opened, lambda: take_a(z, True), arrived, crossed,
    )

    def target(p):
        return far.at[pl.ds(pl.multiple_of(p * points, points), points), :]

    swap(nn, n, narrow_peer, target, far_slots.at[n], sems_far, far_slots.at[0 : nn - 1], True)
    far_slots[n] = far[pl.ds(pl.multiple_of(n * points, points), points), :]
    swap(nn, n, narrow_peer, target, far_slots.at[n], sems_far, far_slots.at[0 : nn - 1], False)
    far_sum = slots_sum(far_slots, nn)
    image = jnp.concatenate(
        [
            0.5 * window[HALF : HALF + points, a * size : (a + 1) * size].astype(f32)
            + far_sum[:, a * size : (a + 1) * size]
            + near[a * points : (a + 1) * points, :]
            for a in range(2)
        ],
        axis=0,
    )

    spread = column(weight_ref[...], points)
    scale = jnp.concatenate([spread, spread], axis=0)
    weighted = image * scale
    for j in range(blocks):
        send_h[j * size : (j + 1) * size, :] = mm(basis_ref[j], weighted, ((0,), (0,)))
    def chunk(ref, p, rows):
        return ref.at[pl.ds(pl.multiple_of(p * rows, rows), rows), :]

    def first(ref, count, rows):
        return ref.at[0 : (count - 1) * rows, :]

    def reduce(count, me, device, src, slots, sems):
        piece = slots.shape[1]
        whole = slots.at[0 : count - 1]
        pick = (lambda p: chunk(src, p, piece)) if src.shape[0] > piece else (lambda p: src)
        swap(count, me, device, pick, slots.at[me], sems, whole, True)
        slots[me] = pick(me)[...]
        swap(count, me, device, pick, slots.at[me], sems, whole, False)
        return slots_sum(slots, count)

    tall_step, step = blocks * size // nz, blocks * size // nw
    mid_z[...] = reduce(nz, z, z_peer, send_h, slots_z, sems_hz)
    mid_h[...] = reduce(nx, x, x_peer, mid_z, slots_x, sems_hx)
    block_z = chunk(full_h, z, tall_step)
    block_z[pl.ds(pl.multiple_of(x * step, step), step), :] = reduce(nn, n, narrow_peer, mid_h, slots_n, sems_n)
    mine = full_h.at[pl.ds(pl.multiple_of(z * tall_step + x * step, step), step), :]
    exchange(nx, x, x_peer, lambda p: mine, mine, sems_hx2, first(full_h, nx, step))
    exchange(nz, z, z_peer, lambda p: block_z, block_z, sems_hz2, first(full_h, nz, tall_step))
    out_h = pltpu.make_async_copy(full_h, hess_ref, sems_io.at[3])
    out_h.start()
    remainder = image
    for j in range(blocks):
        part = full_h[j * size : (j + 1) * size, :]
        remainder = remainder - mm(basis_ref[j], part, ((1,), (0,)))
    rest[...] = remainder
    out_rest = pltpu.make_async_copy(rest, rest_ref, sems_io.at[4])
    out_rest.start()
    send_g[...] = mm(remainder * scale, remainder, ((0,), (0,)))
    gstep = size // nz
    mid_g[...] = reduce(nz, z, z_peer, send_g, slots_gz, sems_z)
    mid_g2[...] = reduce(nx, x, x_peer, mid_g, slots_gx, sems_x)
    full_g[pl.ds(pl.multiple_of(z * gstep, gstep), gstep), :] = reduce(nn, n, narrow_peer, mid_g2, slots_gn, sems_gn)
    exchange(nz, z, z_peer, lambda p: chunk(full_g, z, gstep), chunk(full_g, z, gstep), sems_z2, first(full_g, nz, gstep))
    gram_ref[...] = full_g[...]
    out_h.wait()
    out_rest.wait()


def whole_step(panel, count, points, weight, basis, jacobi, agg, block, inverse, nn, nw, nz):
    blocks, rows, size = basis.shape
    f32, bf16 = jnp.float32, jnp.bfloat16
    pts = weight.shape[1]
    coarse = inverse.shape[1]
    vmem = pl.BlockSpec(memory_space=pltpu.VMEM)
    smem = pl.BlockSpec(memory_space=pltpu.SMEM)
    hbm = pl.BlockSpec(memory_space=pl.ANY)
    step, gstep, nx = blocks * size // nw, size // nz, nw // nz
    chunks, cols = nz + 2 * nx, nx * HALF
    dma = lambda *c: pltpu.SemaphoreType.DMA(c)
    lanes = max(nx // 2, 1)
    buf = pltpu.VMEM
    gather_sems = (dma(2), dma(3), dma(lanes, nz // 2), dma(nz // 2), dma(nz // 2 + 2))
    return pl.pallas_call(
        functools.partial(step_kernel, nn, nw, nz),
        name="step",
        out_shape=(
            jax.ShapeDtypeStruct((rows, size), f32),
            jax.ShapeDtypeStruct((blocks * size, size), f32),
            jax.ShapeDtypeStruct((size, size), f32),
        ),
        in_specs=[smem] * 2 + [vmem] * 2 + [hbm] + [vmem] * 2 + [hbm] * 2,
        out_specs=(hbm, hbm, vmem),
        scratch_shapes=[
            buf(basis.shape, f32),
            buf(block.shape, bf16),
            buf(inverse.shape, f32),
            buf((8, pts), f32),
            buf((nz, nx, 8, pts), f32),
            buf((nn, 8, pts), f32),
            buf((chunks, nx // 2, 8, pts), f32),
            buf((nn, 2, pts, pts), f32),
            buf((chunks, 3, nn * pts, cols), bf16),
            buf((nz, nx, coarse // 2, size), f32),
            buf((nx, nz, coarse // 2, size), f32),
            buf((nx, nz, coarse, size), f32),
            buf((nn, coarse, size), f32),
            buf((nn, coarse, size), f32),
            buf((nz, nx, HALF, 2 * size), bf16),
            buf((nx, nz, HALF, 2 * size), bf16),
            buf((pts + 2 * HALF, 2 * size), bf16),
            buf((2, HALF, 2 * size), bf16),
            buf((nn * pts, 2 * size), f32),
            buf((nn, pts, 2 * size), f32),
            buf((rows, size), f32),
            buf((blocks * size, size), f32),
            buf((nz, nx * step, size), f32),
            buf((nx * step, size), f32),
            buf((nx, step, size), f32),
            buf((step, size), f32),
            buf((nn, step, size), f32),
            buf((blocks * size, size), f32),
            buf((size, size), f32),
            buf((nz, gstep, size), f32),
            buf((gstep, size), f32),
            buf((nx, gstep, size), f32),
            buf((gstep, size), f32),
            buf((nn, gstep, size), f32),
            buf((size, size), f32),
            buf((rows, size), f32),
            pltpu.SemaphoreType.DMA((5,)),
            *([dma(2)] * 4), dma(2, 2),
            *gather_sems, *gather_sems,
            *([dma(2)] * 10),
        ],
        compiler_params=pltpu.CompilerParams(
            collective_id=0, has_side_effects=True, vmem_limit_bytes=60 * 1024 * 1024
        ),
    )(panel, count, points, weight, basis, jacobi, agg, block, inverse)


def finish_kernel(gram_ref, rest_hbm, hess_hbm, new_ref, hess_out, upper_ref, rest, hess, work, sems):
    size = gram_ref.shape[0]
    get_rest = pltpu.make_async_copy(rest_hbm, rest, sems.at[0])
    get_hess = pltpu.make_async_copy(hess_hbm, hess, sems.at[1])
    put_hess = pltpu.make_async_copy(hess, hess_out, sems.at[2])
    get_rest.start()
    get_hess.start()
    get_hess.wait()
    put_hess.start()
    factor(gram_ref[...], work)
    row = lax.broadcasted_iota(jnp.int32, (size, size), 0)
    col = lax.broadcasted_iota(jnp.int32, (size, size), 1)
    upper_ref[...] = jnp.where(row <= col, work[:, 0:size], 0.0)
    get_rest.wait()
    new_ref[...] = mm(rest[...], work[:, size:], ((1,), (1,)))
    put_hess.wait()


def finish(gram, rest, hess):
    f32 = jnp.float32
    size = gram.shape[0]
    vmem = pl.BlockSpec(memory_space=pltpu.VMEM)
    hbm = pl.BlockSpec(memory_space=pl.ANY)
    return pl.pallas_call(
        finish_kernel,
        name="finish",
        out_shape=(
            jax.ShapeDtypeStruct(rest.shape, f32),
            jax.ShapeDtypeStruct(hess.shape, f32),
            jax.ShapeDtypeStruct(gram.shape, f32),
        ),
        in_specs=[vmem, hbm, hbm],
        out_specs=(vmem, hbm, vmem),
        scratch_shapes=[
            pltpu.VMEM(rest.shape, f32),
            pltpu.VMEM(hess.shape, f32),
            pltpu.VMEM((size, 2 * size), f32),
            pltpu.SemaphoreType.DMA((3,)),
        ],
    )(gram, rest, hess)


def body(
    points, quad_weight, basis, jacobi, near_panel, near_count, near_block, agg_index, coarse_inverse, nz=NZ
):
    block_total, comps, point_count, rhs_count = basis.shape
    rest, hess, gram = whole_step(
        near_panel,
        near_count,
        points,
        quad_weight[None, :],
        basis.reshape(block_total, comps * point_count, rhs_count),
        jacobi,
        agg_index,
        near_block,
        coarse_inverse,
        lax.axis_size("narrow"),
        lax.axis_size("wide"),
        nz,
    )
    new_flat, hess, upper = finish(gram, rest, hess)
    return (
        new_flat.reshape(comps, point_count, rhs_count),
        hess.reshape(block_total, rhs_count, rhs_count),
        upper,
    )


def solution(mesh):
    in_specs = (
        P(None, ("narrow", "wide")),
        P(("narrow", "wide")),
        P(None, None, ("narrow", "wide"), None),
        P(None, ("narrow", "wide")),
        P(("narrow", "wide"), None),
        P(("narrow", "wide")),
        P(("narrow", "wide"), None, None, None),
        P(None, ("narrow", "wide")),
        P(None, "wide", "narrow"),
    )
    out_specs = (P(None, ("narrow", "wide"), None), P(), P())
    return jax.shard_map(body, mesh=mesh, in_specs=in_specs, out_specs=out_specs, check_vma=False)
```

```python
import functools

import jax
import jax.numpy as jnp
from jax import lax
from jax.experimental import pallas as pl
from jax.experimental.pallas import tpu as pltpu
from jax.sharding import PartitionSpec as P

NU = 0.3
DELTA2 = 1e-05
ELASTIC = 40.0
HIGH = lax.Precision.HIGHEST
MESH = pl.DeviceIdType.MESH
NZ = 8
PANEL = 32
GROUP = 8
HALF = 64


def mm(a, b, dims):
    return lax.dot_general(a, b, (dims, ((), ())), precision=HIGH, preferred_element_type=jnp.float32)


def drain(sem, ref):
    pltpu.make_async_copy(ref, ref, sem).wait()


def swap(count, me, device, src, dst, sems, whole, go):
    if not go:
        drain(sems.at[0], whole)
        drain(sems.at[1], whole)
        return

    def one(k, carry):
        peer = lax.rem(me + k, count)
        pltpu.make_async_remote_copy(
            src_ref=src(peer),
            dst_ref=dst,
            send_sem=sems.at[0],
            recv_sem=sems.at[1],
            device_id=device(peer),
            device_id_type=MESH,
        ).start()
        return carry

    lax.fori_loop(1, count, one, 0)


def exchange(count, me, device, src, dst, sems, whole):
    swap(count, me, device, src, dst, sems, whole, True)
    swap(count, me, device, src, dst, sems, whole, False)


def ring(count, me, device, block, half, send_sem, recv_sem, step):
    back = step - 1
    for way, peer, origin in ((0, me + 1, me + count - back), (1, me + count - 1, me + back)):
        peer, origin = lax.rem(peer, count), lax.rem(origin, count)
        ref = half(origin, way) if step == count // 2 else block(origin)
        pltpu.make_async_remote_copy(
            src_ref=ref,
            dst_ref=ref,
            send_sem=send_sem,
            recv_sem=recv_sem,
            device_id=device(peer),
            device_id_type=MESH,
        ).start()


def slots_sum(ref, count):
    total = ref[0]
    for k in range(1, count):
        total = total + ref[k]
    return total


def greet(groups, others):
    barrier = pltpu.get_barrier_semaphore()
    for count, me, device in groups:

        def one(k, carry):
            pl.semaphore_signal(barrier, inc=1, device_id=device(lax.rem(me + k, count)), device_id_type=MESH)
            return carry

        lax.fori_loop(1, count, one, 0)
    for peer in others:
        pl.semaphore_signal(barrier, inc=1, device_id=peer, device_id_type=MESH)
    return barrier, sum(count - 1 for count, _, _ in groups) + len(others)


def factor(gram, work):
    size = gram.shape[0]
    rows = lax.broadcasted_iota(jnp.int32, (size, size), 0)
    cols = lax.broadcasted_iota(jnp.int32, (size, size), 1)
    work[:, 0:size] = gram
    work[:, size:] = (rows == cols).astype(jnp.float32)
    sub = lax.broadcasted_iota(jnp.int32, (PANEL, size), 0)
    for base in range(0, size, PANEL):
        sides = [work[base : base + PANEL, 0:size], work[base : base + PANEL, size:]]
        for k in range(0, PANEL, GROUP):
            lefts = [
                jnp.broadcast_to(sides[0][:, base + k + j : base + k + j + 1], (PANEL, size)) for j in range(GROUP)
            ]
            tops = [[side[k + j : k + j + 1, :] for side in sides] for j in range(GROUP)]
            for j in range(GROUP):
                inv = lax.rsqrt(lefts[j][k + j : k + j + 1, :])
                lefts[j] = lefts[j] * inv
                tops[j] = [top * inv for top in tops[j]]
                for i in range(j + 1, GROUP):
                    share = lefts[j][k + i : k + i + 1, :]
                    lefts[i] = lefts[i] - lefts[j] * share
                    tops[i] = [top - share * done for top, done in zip(tops[i], tops[j])]
            for s in range(2):
                new = sides[s]
                for j in range(GROUP):
                    new = new - lefts[j] * tops[j][s]
                new = jnp.where(sub >= k + GROUP, new, sides[s])
                for j in range(GROUP):
                    new = jnp.where(sub == k + j, tops[j][s], new)
                sides[s] = new
        work[base : base + PANEL, 0:size] = sides[0]
        work[base : base + PANEL, size:] = sides[1]
        if base + PANEL < size:
            panel = jnp.concatenate(sides, axis=1)
            below = mm(sides[0], panel, ((0,), (0,)))
            work[base + PANEL :, :] = work[base + PANEL :, :] - below[base + PANEL :, :]


def column(row, points):
    return jnp.transpose(jnp.broadcast_to(row, (points, points)))


def step_kernel(
    nn, nw, nz,
    panel_ref, count_ref, points_ref, weight_ref, basis_hbm, jacobi_ref, agg_ref, block_hbm, inverse_hbm,
    rest_ref, hess_ref, gram_ref,
    basis_ref, block_ref, inverse_ref,
    info, info_w, info_n, sources, columns, green,
    rhs_a, rhs_b, rhs_all, parts, part_slots, fields_a, fields_b, window, halo, far, far_slots, near,
    send_h, slots_n, mid_n, slots_x, mid_h, slots_z, full_h,
    send_g, slots_gn, mid_g, slots_gx, mid_g2, slots_gz, full_g,
    rest,
    sems_io, sems_ix, sems_iz, sems_in, sems_cn, sems_halo,
    sems_cax, sems_cs, sems_caz, sems_cbz, sems_cbx,
    sems_ax, sems_as, sems_az, sems_bz, sems_bx, sems_far,
    sems_n, sems_hx, sems_hz, sems_hx2, sems_n2, sems_gn, sems_x, sems_z, sems_gn2,
):
    f32, bf16 = jnp.float32, jnp.bfloat16
    n = lax.axis_index("narrow")
    w = lax.axis_index("wide")
    x, z = w // nz, lax.rem(w, nz)
    nx = nw // nz
    blocks, size = basis_ref.shape[0], basis_ref.shape[2]
    points = weight_ref.shape[1]
    coarse = inverse_ref.shape[1]
    flat = n * nw + w
    total = nn * nw

    def flat_peer(p):
        return {"narrow": p // nw, "wide": lax.rem(p, nw)}

    before, after = flat_peer(lax.rem(flat + total - 1, total)), flat_peer(lax.rem(flat + 1, total))
    def narrow_peer(p):
        return {"narrow": p}

    def z_peer(p):
        return {"wide": x * nz + p}

    def x_peer(p):
        return {"wide": p * nz + z}

    barrier, greeted = greet(((nn, n, narrow_peer), (nx, x, x_peer), (nz, z, z_peer)), (before, after))
    loads = [
        pltpu.make_async_copy(src, dst, sems_io.at[i])
        for i, (src, dst) in enumerate(((basis_hbm, basis_ref), (inverse_hbm, inverse_ref), (block_hbm, block_ref)))
    ]
    for load in loads:
        load.start()

    lanes = max(nx // 2, 1)

    def gathering(buf_a, buf_b, cut, sem_ax, sem_send, sem_az, sem_bz, sem_bx):
        deep, cross = nz // 2, nx // 2

        def a_first(go):
            swap(nx, x, x_peer, lambda p: buf_a.at[z, x], buf_a.at[z, x], sem_ax, buf_a.at[0, 0 : nx - 1], go)

        def a_ring(j, step, go):
            if not go:
                drain(sem_az.at[j, step - 1], buf_a.at[0:2, 0:2] if step < deep else buf_a.at[0, 0:2])
                return
            ring(
                nz, z, z_peer,
                lambda p: buf_a.at[p, 2 * j : 2 * j + 2],
                lambda p, way: buf_a.at[p, 2 * j + way],
                sem_send.at[0], sem_az.at[j, step - 1], step,
            )

        def part(ref, way):
            return ref.at[:cut] if way == 0 else ref.at[cut:]

        def b_ring(step, go):
            if not go:
                drain(sem_bz.at[step - 1], buf_b.at[0, 0:2] if step < deep else buf_b.at[0, 0])
                return
            ring(
                nz, z, z_peer,
                lambda p: buf_b.at[x, p],
                lambda p, way: part(buf_b.at[x, p], way),
                sem_send.at[1], sem_bz.at[step - 1], step,
            )

        def bx_ring(shift, step, go):
            signs = [sign for at, sign in ((2 * shift - 1, -1), (2 * shift, 1)) if 0 <= at < nz]
            if not go:
                drain(sem_bx.at[shift], buf_b.at[0, 0 : len(signs) * (2 if step < cross else 1)])
                return
            for sign in signs:
                q = lax.rem(z + nz + sign * shift, nz)
                ring(
                    nx, x, x_peer,
                    lambda p: buf_b.at[p, q],
                    lambda p, way: part(buf_b.at[p, q], way),
                    sem_send.at[2], sem_bx.at[shift if step == 1 else deep + 1], step,
                )

        def close():
            if cross > 1:
                drain(sem_bx.at[deep + 1], buf_b.at[0])
            drain(sem_send.at[0], buf_a.at[0 : nz - 1])
            drain(sem_send.at[1], buf_b.at[0, 0 : nz - 1])
            drain(sem_send.at[2], buf_b.at[0 : nx - 1])

        return a_first, a_ring, b_ring, bx_ring, close

    def run_gather(steps, opened, own, arrived, crossed):
        a_first, a_ring, b_ring, bx_ring, close = steps
        deep, wide_steps = nz // 2, nx // 2

        def next_b(step):
            b_ring(step, False)
            if step < deep:
                b_ring(step + 1, True)
            bx_ring(step, 1, True)

        def next_x(shift):
            bx_ring(shift, 1, False)
            if wide_steps > 1:
                bx_ring(shift, 2, True)

        a_first(True)
        b_ring(1, True)
        bx_ring(0, 1, True)
        opened()
        a_first(False)
        for j in range(lanes):
            a_ring(j, 1, True)
        next_b(1)
        next_x(0)
        own()
        if deep > 1:
            next_b(2)
        for step in range(1, deep + 1):
            for j in range(lanes):
                a_ring(j, step, False)
                if step < deep:
                    a_ring(j, step + 1, True)
            if step + 2 <= deep:
                next_b(step + 2)
            if step < deep:
                next_x(step)
            if step == deep - 1:
                next_x(deep)
            arrived(step)
            if step == max(1, deep - 2):
                crossed(0)
            if step == deep - 1:
                crossed(1)
        close()
        if wide_steps > 1:
            crossed(2)

    info[...] = jnp.zeros_like(info)
    info[0:2, :] = points_ref[...]
    info[2:3, :] = ELASTIC * weight_ref[...]
    info_n[n] = info[...]
    info_w[z, x] = info[...]

    ids = lax.broadcasted_iota(jnp.int32, (coarse, points), 0)
    member = [(ids == agg_ref[a : a + 1, :]).astype(f32) for a in range(2)]
    loads[0].wait()
    newest = [basis_ref[blocks - 1, a * points : (a + 1) * points, :] for a in range(2)]
    rhs = mm(member[0], newest[0], ((1,), (0,))) + mm(member[1], newest[1], ((1,), (0,)))
    rhs_a[z, x] = rhs[0 : coarse // 2, :]
    rhs_b[x, z] = rhs[coarse // 2 :, :]
    pl.semaphore_wait(barrier, greeted)
    swap(nx, x, x_peer, lambda p: info, info_w.at[z, x], sems_ix, info_w.at[0, 0 : nx - 1], True)
    swap(nn, n, narrow_peer, lambda p: info, info_n.at[n], sems_in, info_n.at[0 : nn - 1], True)
    chunks = nz + 2 * nx
    tall = 32
    pairs = nx // 2

    def spread_info():
        swap(nx, x, x_peer, lambda p: info, info_w.at[z, x], sems_ix, info_w.at[0, 0 : nx - 1], False)
        swap(nz, z, z_peer, lambda p: info_w.at[z], info_w.at[z], sems_iz, info_w.at[0 : nz - 1], True)

    def prepare():
        swap(nn, n, narrow_peer, lambda p: info, info_n.at[n], sems_in, info_n.at[0 : nn - 1], False)
        swap(nz, z, z_peer, lambda p: info_w.at[z], info_w.at[z], sems_iz, info_w.at[0 : nz - 1], False)
        lane = lax.broadcasted_iota(jnp.int32, (8, points), 1)
        for p in range(nz):
            for m in range(pairs):
                one, two = info_w[p, 2 * m], info_w[p, 2 * m + 1]
                sources[p, m] = jnp.where(lane < HALF, one, pltpu.roll(two, HALF, 1))
        for p in range(nx):
            for h in range(2):
                for m in range(pairs):
                    at = h * (nz // 2) + 2 * m
                    one, two = info_w[at, p], info_w[at + 1, p]
                    sources[nz + 2 * p + h, m] = jnp.where(lane < HALF, pltpu.roll(one, HALF, 1), two)
        for t in range(nn):
            tile = info_n[t]
            for a in range(2):
                columns[t, a] = column(tile[a : a + 1, :], points)

    def evaluate(first, last):
        def unit(i, carry):
            c, t = i // nn, lax.rem(i, nn)
            for m in range(pairs):
                src = sources[c, m]
                sx, sy, sw = src[0:1, :], src[1:2, :], src[2:3, :]
                for r in range(0, points, tall):
                    dx = columns[t, 0, r : r + tall, :] - sx
                    dy = columns[t, 1, r : r + tall, :] - sy
                    xx, yy = dx * dx, dy * dy
                    square = xx + yy + DELTA2
                    inv = 1.0 / square
                    log_part = (-0.5 * (3.0 - 4.0 * NU)) * jnp.log(square)
                    rows = pl.ds(pl.multiple_of(t * points + r, tall), tall)
                    cols = slice(m * points, (m + 1) * points)
                    green[c, 0, rows, cols] = (sw * (log_part + xx * inv)).astype(bf16)
                    green[c, 1, rows, cols] = (sw * (dx * dy * inv)).astype(bf16)
                    green[c, 2, rows, cols] = (sw * (log_part + yy * inv)).astype(bf16)
            return carry

        lax.fori_loop(first, last, unit, 0)

    done = [0]

    def fill(share):
        last = min(done[0] + share * chunks * nn // 128, chunks * nn)
        evaluate(done[0], last)
        done[0] = last

    run_gather(
        gathering(rhs_a, rhs_b, 16, sems_cax, sems_cs, sems_caz, sems_cbz, sems_cbx),
        spread_info, prepare, lambda step: fill(20), lambda step: None,
    )
    for p in range(nx):
        for q in range(nz):
            rhs_all[p, q, 0 : coarse // 2, :] = rhs_a[q, p]
            rhs_all[p, q, coarse // 2 :, :] = rhs_b[p, q]
    loads[1].wait()

    inverse = inverse_ref[...].reshape(nn * coarse, nw * coarse)
    parts[...] = mm(inverse, rhs_all[...].reshape(nw * coarse, size), ((1,), (0,))).reshape(nn, coarse, size)
    swap(nn, n, narrow_peer, lambda p: parts.at[p], part_slots.at[n], sems_cn, part_slots.at[0 : nn - 1], True)
    part_slots[n] = parts[n]
    fill(36)
    swap(nn, n, narrow_peer, lambda p: parts.at[p], part_slots.at[n], sems_cn, part_slots.at[0 : nn - 1], False)
    sol = slots_sum(part_slots, nn)
    for a in range(2):
        lifted = mm(member[a], sol, ((0,), (0,)))
        field = (column(jacobi_ref[a : a + 1, :], points) * newest[a] + lifted).astype(bf16)
        window[HALF : HALF + points, a * size : (a + 1) * size] = field
    fields_a[z, x] = window[HALF : 2 * HALF, :]
    fields_b[x, z] = window[2 * HALF : 3 * HALF, :]

    def halo_copy(way, src, peer, go):
        copy = pltpu.make_async_remote_copy(
            src_ref=src, dst_ref=halo.at[way], send_sem=sems_halo.at[0, way], recv_sem=sems_halo.at[1, way],
            device_id=peer, device_id_type=MESH,
        )
        if go:
            copy.start()
        else:
            copy.wait()

    def halos(go):
        halo_copy(0, fields_b.at[x, z], after, go)
        halo_copy(1, fields_a.at[z, x], before, go)

    def accumulate(c, field, first):
        left, right = field[:, 0:size], field[:, size:]

        def rows_of(i, carry):
            rows = pl.ds(pl.multiple_of(i * 2 * points, 2 * points), 2 * points)
            cross = jnp.dot(green[c, 1, rows, :], field, preferred_element_type=f32)
            one = jnp.dot(green[c, 0, rows, :], left, preferred_element_type=f32) + cross[:, size:]
            two = jnp.dot(green[c, 2, rows, :], right, preferred_element_type=f32) + cross[:, 0:size]
            if first:
                far[rows, 0:size] = one
                far[rows, size:] = two
            else:
                far[rows, 0:size] = far[rows, 0:size] + one
                far[rows, size:] = far[rows, size:] + two
            return carry

        lax.fori_loop(0, nn // 2, rows_of, 0)

    def take_a(p, first=False):
        p = lax.rem(p, nz)
        accumulate(p, fields_a[p].reshape(nx * HALF, 2 * size), first)

    def take_b(p):
        p = lax.rem(p, nx)
        for h in range(2):
            part = fields_b[p, h * (nz // 2) : (h + 1) * (nz // 2)]
            accumulate(nz + 2 * p + h, part.reshape(nz // 2 * HALF, 2 * size), False)

    def near_field():
        halos(False)
        loads[2].wait()
        window[0:HALF, :] = halo[0]
        window[HALF + points :, :] = halo[1]
        q = block_ref.shape[2] // 2
        panels, slots = block_ref.shape[0], block_ref.shape[1]

        reach = points + 2 * HALF
        row_id = lax.broadcasted_iota(jnp.int32, (q, reach), 0)
        col_id = lax.broadcasted_iota(jnp.int32, (q, reach), 1)

        def one_panel(p, carry):
            live = jnp.full((q, reach), count_ref[p], jnp.int32)
            picks = []
            for k in range(slots):
                start = jnp.full((q, reach), (panel_ref[p, k] - flat * panels) * q + HALF, jnp.int32)
                picks.append(((col_id == start + row_id) & (live > k)).astype(f32))
            pick = jnp.concatenate(picks, axis=0).astype(bf16)
            rows = jnp.dot(pick, window[...], preferred_element_type=f32).astype(bf16)
            total = jnp.zeros((2 * q, size), f32)
            for k in range(slots):
                one = rows[k * q : (k + 1) * q, :]
                both = jnp.concatenate([one[:, 0:size], one[:, size:]], axis=0)
                total = total + jnp.dot(block_ref[p, k], both, preferred_element_type=f32)
            for a in range(2):
                near[pl.ds(pl.multiple_of(a * points + p * q, q), q), :] = total[a * q : (a + 1) * q, :]
            return carry

        lax.fori_loop(0, panels, one_panel, 0)

    def opened():
        halos(True)
        fill(12)

    def arrived(step):
        fill(128)
        take_a(z + nz - step)
        if step < nz // 2:
            take_a(z + step)
        if step == 1:
            near_field()

    def crossed(step):
        if step == 0:
            take_b(x)
            return
        take_b(x + nx - step)
        if step < nx // 2:
            take_b(x + step)

    run_gather(
        gathering(fields_a, fields_b, HALF // 2, sems_ax, sems_as, sems_az, sems_bz, sems_bx),
        opened, lambda: take_a(z, True), arrived, crossed,
    )

    def target(p):
        return far.at[pl.ds(pl.multiple_of(p * points, points), points), :]

    swap(nn, n, narrow_peer, target, far_slots.at[n], sems_far, far_slots.at[0 : nn - 1], True)
    far_slots[n] = far[pl.ds(pl.multiple_of(n * points, points), points), :]
    swap(nn, n, narrow_peer, target, far_slots.at[n], sems_far, far_slots.at[0 : nn - 1], False)
    far_sum = slots_sum(far_slots, nn)
    image = jnp.concatenate(
        [
            0.5 * window[HALF : HALF + points, a * size : (a + 1) * size].astype(f32)
            + far_sum[:, a * size : (a + 1) * size]
            + near[a * points : (a + 1) * points, :]
            for a in range(2)
        ],
        axis=0,
    )

    spread = column(weight_ref[...], points)
    scale = jnp.concatenate([spread, spread], axis=0)
    weighted = image * scale
    for j in range(blocks):
        send_h[j * size : (j + 1) * size, :] = mm(basis_ref[j], weighted, ((0,), (0,)))
    def chunk(ref, p, rows):
        return ref.at[pl.ds(pl.multiple_of(p * rows, rows), rows), :]

    def first(ref, count, rows):
        return ref.at[0 : (count - 1) * rows, :]

    def reduce(count, me, device, src, slots, sems):
        piece = slots.shape[1]
        whole = slots.at[0 : count - 1]
        pick = (lambda p: chunk(src, p, piece)) if src.shape[0] > piece else (lambda p: src)
        swap(count, me, device, pick, slots.at[me], sems, whole, True)
        slots[me] = pick(me)[...]
        swap(count, me, device, pick, slots.at[me], sems, whole, False)
        return slots_sum(slots, count)

    wide_piece, piece = blocks * size // nn, blocks * size // nn // nx
    mid_n[...] = reduce(nn, n, narrow_peer, send_h, slots_n, sems_n)
    mid_h[...] = reduce(nx, x, x_peer, mid_n, slots_x, sems_hx)
    mine = full_h.at[pl.ds(pl.multiple_of(n * wide_piece + x * piece, piece), piece), :]
    mine[...] = reduce(nz, z, z_peer, mid_h, slots_z, sems_hz)
    exchange(nx, x, x_peer, lambda p: mine, mine, sems_hx2, first(full_h, nx, piece))
    block_n = chunk(full_h, n, wide_piece)
    exchange(nn, n, narrow_peer, lambda p: block_n, block_n, sems_n2, first(full_h, nn, wide_piece))
    out_h = pltpu.make_async_copy(full_h, hess_ref, sems_io.at[3])
    out_h.start()
    remainder = image
    for j in range(blocks):
        part = full_h[j * size : (j + 1) * size, :]
        remainder = remainder - mm(basis_ref[j], part, ((1,), (0,)))
    rest[...] = remainder
    out_rest = pltpu.make_async_copy(rest, rest_ref, sems_io.at[4])
    out_rest.start()
    send_g[...] = mm(remainder * scale, remainder, ((0,), (0,)))
    gstep = size // nn
    mid_g[...] = reduce(nn, n, narrow_peer, send_g, slots_gn, sems_gn)
    mid_g2[...] = reduce(nx, x, x_peer, mid_g, slots_gx, sems_x)
    own_g = chunk(full_g, n, gstep)
    own_g[...] = reduce(nz, z, z_peer, mid_g2, slots_gz, sems_z)
    exchange(nn, n, narrow_peer, lambda p: own_g, own_g, sems_gn2, first(full_g, nn, gstep))
    gram_ref[...] = full_g[...]
    out_h.wait()
    out_rest.wait()


def whole_step(panel, count, points, weight, basis, jacobi, agg, block, inverse, nn, nw, nz):
    blocks, rows, size = basis.shape
    f32, bf16 = jnp.float32, jnp.bfloat16
    pts = weight.shape[1]
    coarse = inverse.shape[1]
    vmem = pl.BlockSpec(memory_space=pltpu.VMEM)
    smem = pl.BlockSpec(memory_space=pltpu.SMEM)
    hbm = pl.BlockSpec(memory_space=pl.ANY)
    nx = nw // nz
    step, gstep = blocks * size // nn // nx, size // nn
    chunks, cols = nz + 2 * nx, nx * HALF
    dma = lambda *c: pltpu.SemaphoreType.DMA(c)
    lanes = max(nx // 2, 1)
    buf = pltpu.VMEM
    gather_sems = (dma(2), dma(3), dma(lanes, nz // 2), dma(nz // 2), dma(nz // 2 + 2))
    return pl.pallas_call(
        functools.partial(step_kernel, nn, nw, nz),
        name="step",
        out_shape=(
            jax.ShapeDtypeStruct((rows, size), f32),
            jax.ShapeDtypeStruct((blocks * size, size), f32),
            jax.ShapeDtypeStruct((size, size), f32),
        ),
        in_specs=[smem] * 2 + [vmem] * 2 + [hbm] + [vmem] * 2 + [hbm] * 2,
        out_specs=(hbm, hbm, vmem),
        scratch_shapes=[
            buf(basis.shape, f32),
            buf(block.shape, bf16),
            buf(inverse.shape, f32),
            buf((8, pts), f32),
            buf((nz, nx, 8, pts), f32),
            buf((nn, 8, pts), f32),
            buf((chunks, nx // 2, 8, pts), f32),
            buf((nn, 2, pts, pts), f32),
            buf((chunks, 3, nn * pts, cols), bf16),
            buf((nz, nx, coarse // 2, size), f32),
            buf((nx, nz, coarse // 2, size), f32),
            buf((nx, nz, coarse, size), f32),
            buf((nn, coarse, size), f32),
            buf((nn, coarse, size), f32),
            buf((nz, nx, HALF, 2 * size), bf16),
            buf((nx, nz, HALF, 2 * size), bf16),
            buf((pts + 2 * HALF, 2 * size), bf16),
            buf((2, HALF, 2 * size), bf16),
            buf((nn * pts, 2 * size), f32),
            buf((nn, pts, 2 * size), f32),
            buf((rows, size), f32),
            buf((blocks * size, size), f32),
            buf((nn, nx * step, size), f32),
            buf((nx * step, size), f32),
            buf((nx, step, size), f32),
            buf((step, size), f32),
            buf((nz, step, size), f32),
            buf((blocks * size, size), f32),
            buf((size, size), f32),
            buf((nn, gstep, size), f32),
            buf((gstep, size), f32),
            buf((nx, gstep, size), f32),
            buf((gstep, size), f32),
            buf((nz, gstep, size), f32),
            buf((size, size), f32),
            buf((rows, size), f32),
            pltpu.SemaphoreType.DMA((5,)),
            *([dma(2)] * 4), dma(2, 2),
            *gather_sems, *gather_sems,
            *([dma(2)] * 10),
        ],
        compiler_params=pltpu.CompilerParams(
            collective_id=0, has_side_effects=True, vmem_limit_bytes=60 * 1024 * 1024
        ),
    )(panel, count, points, weight, basis, jacobi, agg, block, inverse)


def finish_kernel(gram_ref, rest_hbm, hess_hbm, new_ref, hess_out, upper_ref, rest, hess, work, sems):
    size = gram_ref.shape[0]
    get_rest = pltpu.make_async_copy(rest_hbm, rest, sems.at[0])
    get_hess = pltpu.make_async_copy(hess_hbm, hess, sems.at[1])
    put_hess = pltpu.make_async_copy(hess, hess_out, sems.at[2])
    get_rest.start()
    get_hess.start()
    get_hess.wait()
    put_hess.start()
    factor(gram_ref[...], work)
    row = lax.broadcasted_iota(jnp.int32, (size, size), 0)
    col = lax.broadcasted_iota(jnp.int32, (size, size), 1)
    upper_ref[...] = jnp.where(row <= col, work[:, 0:size], 0.0)
    get_rest.wait()
    new_ref[...] = mm(rest[...], work[:, size:], ((1,), (1,)))
    put_hess.wait()


def finish(gram, rest, hess):
    f32 = jnp.float32
    size = gram.shape[0]
    vmem = pl.BlockSpec(memory_space=pltpu.VMEM)
    hbm = pl.BlockSpec(memory_space=pl.ANY)
    return pl.pallas_call(
        finish_kernel,
        name="finish",
        out_shape=(
            jax.ShapeDtypeStruct(rest.shape, f32),
            jax.ShapeDtypeStruct(hess.shape, f32),
            jax.ShapeDtypeStruct(gram.shape, f32),
        ),
        in_specs=[vmem, hbm, hbm],
        out_specs=(vmem, hbm, vmem),
        scratch_shapes=[
            pltpu.VMEM(rest.shape, f32),
            pltpu.VMEM(hess.shape, f32),
            pltpu.VMEM((size, 2 * size), f32),
            pltpu.SemaphoreType.DMA((3,)),
        ],
    )(gram, rest, hess)


def body(
    points, quad_weight, basis, jacobi, near_panel, near_count, near_block, agg_index, coarse_inverse, nz=NZ
):
    block_total, comps, point_count, rhs_count = basis.shape
    rest, hess, gram = whole_step(
        near_panel,
        near_count,
        points,
        quad_weight[None, :],
        basis.reshape(block_total, comps * point_count, rhs_count),
        jacobi,
        agg_index,
        near_block,
        coarse_inverse,
        lax.axis_size("narrow"),
        lax.axis_size("wide"),
        nz,
    )
    new_flat, hess, upper = finish(gram, rest, hess)
    return (
        new_flat.reshape(comps, point_count, rhs_count),
        hess.reshape(block_total, rhs_count, rhs_count),
        upper,
    )


def solution(mesh):
    in_specs = (
        P(None, ("narrow", "wide")),
        P(("narrow", "wide")),
        P(None, None, ("narrow", "wide"), None),
        P(None, ("narrow", "wide")),
        P(("narrow", "wide"), None),
        P(("narrow", "wide")),
        P(("narrow", "wide"), None, None, None),
        P(None, ("narrow", "wide")),
        P(None, "wide", "narrow"),
    )
    out_specs = (P(None, ("narrow", "wide"), None), P(), P())
    return jax.shard_map(body, mesh=mesh, in_specs=in_specs, out_specs=out_specs, check_vma=False)
```

```python
import functools

import jax
import jax.numpy as jnp
from jax import lax
from jax.experimental import pallas as pl
from jax.experimental.pallas import tpu as pltpu
from jax.sharding import PartitionSpec as P

NU = 0.3
DELTA2 = 1e-05
ELASTIC = 40.0
HIGH = lax.Precision.HIGHEST
MESH = pl.DeviceIdType.MESH
NZ = 8
PANEL = 32
GROUP = 16
HALF = 64


def mm(a, b, dims):
    return lax.dot_general(a, b, (dims, ((), ())), precision=HIGH, preferred_element_type=jnp.float32)


def drain(sem, ref):
    pltpu.make_async_copy(ref, ref, sem).wait()


def swap(count, me, device, src, dst, sems, whole, go):
    if not go:
        drain(sems.at[0], whole)
        drain(sems.at[1], whole)
        return

    def one(k, carry):
        peer = lax.rem(me + k, count)
        pltpu.make_async_remote_copy(
            src_ref=src(peer),
            dst_ref=dst,
            send_sem=sems.at[0],
            recv_sem=sems.at[1],
            device_id=device(peer),
            device_id_type=MESH,
        ).start()
        return carry

    lax.fori_loop(1, count, one, 0)


def exchange(count, me, device, src, dst, sems, whole):
    swap(count, me, device, src, dst, sems, whole, True)
    swap(count, me, device, src, dst, sems, whole, False)


def ring(count, me, device, block, half, send_sem, recv_sem, step):
    back = step - 1
    for way, peer, origin in ((0, me + 1, me + count - back), (1, me + count - 1, me + back)):
        peer, origin = lax.rem(peer, count), lax.rem(origin, count)
        ref = half(origin, way) if step == count // 2 else block(origin)
        pltpu.make_async_remote_copy(
            src_ref=ref,
            dst_ref=ref,
            send_sem=send_sem,
            recv_sem=recv_sem,
            device_id=device(peer),
            device_id_type=MESH,
        ).start()


def slots_sum(ref, count):
    total = ref[0]
    for k in range(1, count):
        total = total + ref[k]
    return total


def greet(groups, others):
    barrier = pltpu.get_barrier_semaphore()
    for count, me, device in groups:

        def one(k, carry):
            pl.semaphore_signal(barrier, inc=1, device_id=device(lax.rem(me + k, count)), device_id_type=MESH)
            return carry

        lax.fori_loop(1, count, one, 0)
    for peer in others:
        pl.semaphore_signal(barrier, inc=1, device_id=peer, device_id_type=MESH)
    return barrier, sum(count - 1 for count, _, _ in groups) + len(others)


def factor(gram, work):
    size = gram.shape[0]
    rows = lax.broadcasted_iota(jnp.int32, (size, size), 0)
    cols = lax.broadcasted_iota(jnp.int32, (size, size), 1)
    work[:, 0:size] = gram
    work[:, size:] = (rows == cols).astype(jnp.float32)
    sub = lax.broadcasted_iota(jnp.int32, (PANEL, size), 0)
    for base in range(0, size, PANEL):
        sides = [work[base : base + PANEL, 0:size], work[base : base + PANEL, size:]]
        for k in range(0, PANEL, GROUP):
            lefts = [
                jnp.broadcast_to(sides[0][:, base + k + j : base + k + j + 1], (PANEL, size)) for j in range(GROUP)
            ]
            tops = [[side[k + j : k + j + 1, :] for side in sides] for j in range(GROUP)]
            for j in range(GROUP):
                inv = lax.rsqrt(lefts[j][k + j : k + j + 1, :])
                lefts[j] = lefts[j] * inv
                tops[j] = [top * inv for top in tops[j]]
                for i in range(j + 1, GROUP):
                    share = lefts[j][k + i : k + i + 1, :]
                    lefts[i] = lefts[i] - lefts[j] * share
                    tops[i] = [top - share * done for top, done in zip(tops[i], tops[j])]
            for s in range(2):
                new = sides[s]
                for j in range(GROUP):
                    new = new - lefts[j] * tops[j][s]
                new = jnp.where(sub >= k + GROUP, new, sides[s])
                for j in range(GROUP):
                    new = jnp.where(sub == k + j, tops[j][s], new)
                sides[s] = new
        work[base : base + PANEL, 0:size] = sides[0]
        work[base : base + PANEL, size:] = sides[1]
        if base + PANEL < size:
            panel = jnp.concatenate(sides, axis=1)
            below = mm(sides[0], panel, ((0,), (0,)))
            work[base + PANEL :, :] = work[base + PANEL :, :] - below[base + PANEL :, :]


def column(row, points):
    return jnp.transpose(jnp.broadcast_to(row, (points, points)))


def step_kernel(
    nn, nw, nz,
    panel_ref, count_ref, points_ref, weight_ref, basis_hbm, jacobi_ref, agg_ref, block_hbm, inverse_hbm,
    rest_ref, hess_ref, gram_ref,
    basis_ref, block_ref, inverse_ref,
    info, info_w, info_n, sources, columns, green,
    rhs_a, rhs_b, rhs_all, parts, part_slots, fields_a, fields_b, window, halo, far, far_slots, near,
    send_h, slots_n, mid_n, slots_x, mid_h, slots_z, full_h,
    send_g, slots_gn, mid_g, slots_gx, mid_g2, slots_gz, full_g,
    rest,
    sems_io, sems_ix, sems_iz, sems_in, sems_cn, sems_halo,
    sems_cax, sems_cs, sems_caz, sems_cbz, sems_cbx,
    sems_ax, sems_as, sems_az, sems_bz, sems_bx, sems_far,
    sems_n, sems_hx, sems_hz, sems_hx2, sems_n2, sems_gn, sems_x, sems_z, sems_gn2,
):
    f32, bf16 = jnp.float32, jnp.bfloat16
    n = lax.axis_index("narrow")
    w = lax.axis_index("wide")
    x, z = w // nz, lax.rem(w, nz)
    nx = nw // nz
    blocks, size = basis_ref.shape[0], basis_ref.shape[2]
    points = weight_ref.shape[1]
    coarse = inverse_ref.shape[1]
    flat = n * nw + w
    total = nn * nw

    def flat_peer(p):
        return {"narrow": p // nw, "wide": lax.rem(p, nw)}

    before, after = flat_peer(lax.rem(flat + total - 1, total)), flat_peer(lax.rem(flat + 1, total))
    def narrow_peer(p):
        return {"narrow": p}

    def z_peer(p):
        return {"wide": x * nz + p}

    def x_peer(p):
        return {"wide": p * nz + z}

    barrier, greeted = greet(((nn, n, narrow_peer), (nx, x, x_peer), (nz, z, z_peer)), (before, after))
    loads = [
        pltpu.make_async_copy(src, dst, sems_io.at[i])
        for i, (src, dst) in enumerate(((basis_hbm, basis_ref), (inverse_hbm, inverse_ref), (block_hbm, block_ref)))
    ]
    for load in loads:
        load.start()

    lanes = max(nx // 2, 1)

    def gathering(buf_a, buf_b, cut, sem_ax, sem_send, sem_az, sem_bz, sem_bx):
        deep, cross = nz // 2, nx // 2

        def a_first(go):
            swap(nx, x, x_peer, lambda p: buf_a.at[z, x], buf_a.at[z, x], sem_ax, buf_a.at[0, 0 : nx - 1], go)

        def a_ring(j, step, go):
            if not go:
                drain(sem_az.at[j, step - 1], buf_a.at[0:2, 0:2] if step < deep else buf_a.at[0, 0:2])
                return
            ring(
                nz, z, z_peer,
                lambda p: buf_a.at[p, 2 * j : 2 * j + 2],
                lambda p, way: buf_a.at[p, 2 * j + way],
                sem_send.at[0], sem_az.at[j, step - 1], step,
            )

        def part(ref, way):
            return ref.at[:cut] if way == 0 else ref.at[cut:]

        def b_ring(step, go):
            if not go:
                drain(sem_bz.at[step - 1], buf_b.at[0, 0:2] if step < deep else buf_b.at[0, 0])
                return
            ring(
                nz, z, z_peer,
                lambda p: buf_b.at[x, p],
                lambda p, way: part(buf_b.at[x, p], way),
                sem_send.at[1], sem_bz.at[step - 1], step,
            )

        def bx_ring(shift, step, go):
            signs = [sign for at, sign in ((2 * shift - 1, -1), (2 * shift, 1)) if 0 <= at < nz]
            if not go:
                drain(sem_bx.at[shift], buf_b.at[0, 0 : len(signs) * (2 if step < cross else 1)])
                return
            for sign in signs:
                q = lax.rem(z + nz + sign * shift, nz)
                ring(
                    nx, x, x_peer,
                    lambda p: buf_b.at[p, q],
                    lambda p, way: part(buf_b.at[p, q], way),
                    sem_send.at[2], sem_bx.at[shift if step == 1 else deep + 1], step,
                )

        def close():
            if cross > 1:
                drain(sem_bx.at[deep + 1], buf_b.at[0])
            drain(sem_send.at[0], buf_a.at[0 : nz - 1])
            drain(sem_send.at[1], buf_b.at[0, 0 : nz - 1])
            drain(sem_send.at[2], buf_b.at[0 : nx - 1])

        return a_first, a_ring, b_ring, bx_ring, close

    def run_gather(steps, opened, own, arrived, crossed):
        a_first, a_ring, b_ring, bx_ring, close = steps
        deep, wide_steps = nz // 2, nx // 2

        def next_b(step):
            b_ring(step, False)
            if step < deep:
                b_ring(step + 1, True)
            bx_ring(step, 1, True)

        def next_x(shift):
            bx_ring(shift, 1, False)
            if wide_steps > 1:
                bx_ring(shift, 2, True)

        a_first(True)
        b_ring(1, True)
        bx_ring(0, 1, True)
        opened()
        a_first(False)
        for j in range(lanes):
            a_ring(j, 1, True)
        next_b(1)
        next_x(0)
        own()
        if deep > 1:
            next_b(2)
        for step in range(1, deep + 1):
            for j in range(lanes):
                a_ring(j, step, False)
                if step < deep:
                    a_ring(j, step + 1, True)
            if step + 2 <= deep:
                next_b(step + 2)
            if step < deep:
                next_x(step)
            if step == deep - 1:
                next_x(deep)
            arrived(step)
            if step == max(1, deep - 2):
                crossed(0)
            if step == deep - 1:
                crossed(1)
        close()
        if wide_steps > 1:
            crossed(2)

    info[...] = jnp.zeros_like(info)
    info[0:2, :] = points_ref[...]
    info[2:3, :] = ELASTIC * weight_ref[...]
    info_n[n] = info[...]
    info_w[z, x] = info[...]

    ids = lax.broadcasted_iota(jnp.int32, (coarse, points), 0)
    member = [(ids == agg_ref[a : a + 1, :]).astype(f32) for a in range(2)]
    loads[0].wait()
    newest = [basis_ref[blocks - 1, a * points : (a + 1) * points, :] for a in range(2)]
    rhs = mm(member[0], newest[0], ((1,), (0,))) + mm(member[1], newest[1], ((1,), (0,)))
    rhs_a[z, x] = rhs[0 : coarse // 2, :]
    rhs_b[x, z] = rhs[coarse // 2 :, :]
    pl.semaphore_wait(barrier, greeted)
    swap(nx, x, x_peer, lambda p: info, info_w.at[z, x], sems_ix, info_w.at[0, 0 : nx - 1], True)
    swap(nn, n, narrow_peer, lambda p: info, info_n.at[n], sems_in, info_n.at[0 : nn - 1], True)
    chunks = nz + 2 * nx
    tall = 32
    pairs = nx // 2

    def spread_info():
        swap(nx, x, x_peer, lambda p: info, info_w.at[z, x], sems_ix, info_w.at[0, 0 : nx - 1], False)
        swap(nz, z, z_peer, lambda p: info_w.at[z], info_w.at[z], sems_iz, info_w.at[0 : nz - 1], True)

    def prepare():
        swap(nn, n, narrow_peer, lambda p: info, info_n.at[n], sems_in, info_n.at[0 : nn - 1], False)
        swap(nz, z, z_peer, lambda p: info_w.at[z], info_w.at[z], sems_iz, info_w.at[0 : nz - 1], False)
        lane = lax.broadcasted_iota(jnp.int32, (8, points), 1)
        for p in range(nz):
            for m in range(pairs):
                one, two = info_w[p, 2 * m], info_w[p, 2 * m + 1]
                sources[p, m] = jnp.where(lane < HALF, one, pltpu.roll(two, HALF, 1))
        for p in range(nx):
            for h in range(2):
                for m in range(pairs):
                    at = h * (nz // 2) + 2 * m
                    one, two = info_w[at, p], info_w[at + 1, p]
                    sources[nz + 2 * p + h, m] = jnp.where(lane < HALF, pltpu.roll(one, HALF, 1), two)
        for t in range(nn):
            tile = info_n[t]
            for a in range(2):
                columns[t, a] = column(tile[a : a + 1, :], points)

    def evaluate(first, last):
        def unit(i, carry):
            c, t = i // nn, lax.rem(i, nn)
            for m in range(pairs):
                src = sources[c, m]
                sx, sy, sw = src[0:1, :], src[1:2, :], src[2:3, :]
                for r in range(0, points, tall):
                    dx = columns[t, 0, r : r + tall, :] - sx
                    dy = columns[t, 1, r : r + tall, :] - sy
                    xx, yy = dx * dx, dy * dy
                    square = xx + yy + DELTA2
                    inv = 1.0 / square
                    log_part = (-0.5 * (3.0 - 4.0 * NU)) * jnp.log(square)
                    rows = pl.ds(pl.multiple_of(t * points + r, tall), tall)
                    cols = slice(m * points, (m + 1) * points)
                    green[c, 0, rows, cols] = (sw * (log_part + xx * inv)).astype(bf16)
                    green[c, 1, rows, cols] = (sw * (dx * dy * inv)).astype(bf16)
                    green[c, 2, rows, cols] = (sw * (log_part + yy * inv)).astype(bf16)
            return carry

        lax.fori_loop(first, last, unit, 0)

    done = [0]

    def fill(share):
        last = min(done[0] + share * chunks * nn // 128, chunks * nn)
        evaluate(done[0], last)
        done[0] = last

    run_gather(
        gathering(rhs_a, rhs_b, 16, sems_cax, sems_cs, sems_caz, sems_cbz, sems_cbx),
        spread_info, prepare, lambda step: fill(20), lambda step: None,
    )
    for p in range(nx):
        for q in range(nz):
            rhs_all[p, q, 0 : coarse // 2, :] = rhs_a[q, p]
            rhs_all[p, q, coarse // 2 :, :] = rhs_b[p, q]
    loads[1].wait()

    inverse = inverse_ref[...].reshape(nn * coarse, nw * coarse)
    parts[...] = mm(inverse, rhs_all[...].reshape(nw * coarse, size), ((1,), (0,))).reshape(nn, coarse, size)
    swap(nn, n, narrow_peer, lambda p: parts.at[p], part_slots.at[n], sems_cn, part_slots.at[0 : nn - 1], True)
    part_slots[n] = parts[n]
    fill(36)
    swap(nn, n, narrow_peer, lambda p: parts.at[p], part_slots.at[n], sems_cn, part_slots.at[0 : nn - 1], False)
    sol = slots_sum(part_slots, nn)
    for a in range(2):
        lifted = mm(member[a], sol, ((0,), (0,)))
        field = (column(jacobi_ref[a : a + 1, :], points) * newest[a] + lifted).astype(bf16)
        window[HALF : HALF + points, a * size : (a + 1) * size] = field
    fields_a[z, x] = window[HALF : 2 * HALF, :]
    fields_b[x, z] = window[2 * HALF : 3 * HALF, :]

    def halo_copy(way, src, peer, go):
        copy = pltpu.make_async_remote_copy(
            src_ref=src, dst_ref=halo.at[way], send_sem=sems_halo.at[0, way], recv_sem=sems_halo.at[1, way],
            device_id=peer, device_id_type=MESH,
        )
        if go:
            copy.start()
        else:
            copy.wait()

    def halos(go):
        halo_copy(0, fields_b.at[x, z], after, go)
        halo_copy(1, fields_a.at[z, x], before, go)

    def accumulate_rows(c, field, first, i):
        left, right = field[:, 0:size], field[:, size:]
        rows = pl.ds(pl.multiple_of(i * 2 * points, 2 * points), 2 * points)
        cross = jnp.dot(green[c, 1, rows, :], field, preferred_element_type=f32)
        one = jnp.dot(green[c, 0, rows, :], left, preferred_element_type=f32) + cross[:, size:]
        two = jnp.dot(green[c, 2, rows, :], right, preferred_element_type=f32) + cross[:, 0:size]
        if first:
            far[rows, 0:size] = one
            far[rows, size:] = two
        else:
            far[rows, 0:size] = far[rows, 0:size] + one
            far[rows, size:] = far[rows, size:] + two

    def accumulate(c, field, first):
        def rows_of(i, carry):
            accumulate_rows(c, field, first, i)
            return carry

        lax.fori_loop(0, nn // 2, rows_of, 0)

    def send_far(p):
        pltpu.make_async_remote_copy(
            src_ref=far.at[pl.ds(pl.multiple_of(p * points, points), points), :],
            dst_ref=far_slots.at[n],
            send_sem=sems_far.at[0],
            recv_sem=sems_far.at[1],
            device_id=narrow_peer(p),
            device_id_type=MESH,
        ).start()

    def part_b(p, h):
        return fields_b[p, h * (nz // 2) : (h + 1) * (nz // 2)].reshape(nz // 2 * HALF, 2 * size)

    def finish_far(p):
        p = lax.rem(p, nx)
        pairs_of = nn // 2
        for shift in sorted(range(pairs_of), key=lambda k: -min(k, pairs_of - k)):
            i = lax.rem(n // 2 + shift, pairs_of)
            for h in range(2):
                accumulate_rows(nz + 2 * p + h, part_b(p, h), False, i)
            if shift:
                send_far(2 * i)
                send_far(2 * i + 1)
            else:
                send_far(2 * i + 1 - lax.rem(n, 2))

    def take_a(p, first=False):
        p = lax.rem(p, nz)
        accumulate(p, fields_a[p].reshape(nx * HALF, 2 * size), first)

    def take_b(p):
        p = lax.rem(p, nx)
        for h in range(2):
            part = fields_b[p, h * (nz // 2) : (h + 1) * (nz // 2)]
            accumulate(nz + 2 * p + h, part.reshape(nz // 2 * HALF, 2 * size), False)

    def near_field():
        halos(False)
        loads[2].wait()
        window[0:HALF, :] = halo[0]
        window[HALF + points :, :] = halo[1]
        q = block_ref.shape[2] // 2
        panels, slots = block_ref.shape[0], block_ref.shape[1]

        reach = points + 2 * HALF
        row_id = lax.broadcasted_iota(jnp.int32, (q, reach), 0)
        col_id = lax.broadcasted_iota(jnp.int32, (q, reach), 1)

        def one_panel(p, carry):
            live = jnp.full((q, reach), count_ref[p], jnp.int32)
            picks = []
            for k in range(slots):
                start = jnp.full((q, reach), (panel_ref[p, k] - flat * panels) * q + HALF, jnp.int32)
                picks.append(((col_id == start + row_id) & (live > k)).astype(f32))
            pick = jnp.concatenate(picks, axis=0).astype(bf16)
            rows = jnp.dot(pick, window[...], preferred_element_type=f32).astype(bf16)
            total = jnp.zeros((2 * q, size), f32)
            for k in range(slots):
                one = rows[k * q : (k + 1) * q, :]
                both = jnp.concatenate([one[:, 0:size], one[:, size:]], axis=0)
                total = total + jnp.dot(block_ref[p, k], both, preferred_element_type=f32)
            for a in range(2):
                near[pl.ds(pl.multiple_of(a * points + p * q, q), q), :] = total[a * q : (a + 1) * q, :]
            return carry

        lax.fori_loop(0, panels, one_panel, 0)

    def opened():
        halos(True)
        fill(12)

    def arrived(step):
        fill(128)
        take_a(z + nz - step)
        if step < nz // 2:
            take_a(z + step)
        if step == 1:
            near_field()

    def crossed(step):
        if step == 0:
            take_b(x)
            return
        if step == 2:
            finish_far(x + nx - step)
            return
        take_b(x + nx - step)
        if step < nx // 2:
            take_b(x + step)

    run_gather(
        gathering(fields_a, fields_b, HALF // 2, sems_ax, sems_as, sems_az, sems_bz, sems_bx),
        opened, lambda: take_a(z, True), arrived, crossed,
    )

    if nx == 2:
        for shift in range(1, nn):
            send_far(lax.rem(n + shift, nn))
    far_slots[n] = far[pl.ds(pl.multiple_of(n * points, points), points), :]
    base = jnp.concatenate([near[0:points, :], near[points:, :]], axis=1)
    base = base + 0.5 * window[HALF : HALF + points, :].astype(f32)
    drain(sems_far.at[0], far_slots.at[0 : nn - 1])
    drain(sems_far.at[1], far_slots.at[0 : nn - 1])
    base = base + slots_sum(far_slots, nn)
    image = jnp.concatenate([base[:, 0:size], base[:, size:]], axis=0)

    spread = column(weight_ref[...], points)
    scale = jnp.concatenate([spread, spread], axis=0)
    weighted = image * scale
    for j in range(blocks):
        send_h[j * size : (j + 1) * size, :] = mm(basis_ref[j], weighted, ((0,), (0,)))
    def chunk(ref, p, rows):
        return ref.at[pl.ds(pl.multiple_of(p * rows, rows), rows), :]

    def first(ref, count, rows):
        return ref.at[0 : (count - 1) * rows, :]

    def reduce(count, me, device, src, slots, sems):
        piece = slots.shape[1]
        whole = slots.at[0 : count - 1]
        pick = (lambda p: chunk(src, p, piece)) if src.shape[0] > piece else (lambda p: src)
        swap(count, me, device, pick, slots.at[me], sems, whole, True)
        slots[me] = pick(me)[...]
        swap(count, me, device, pick, slots.at[me], sems, whole, False)
        return slots_sum(slots, count)

    wide_piece, piece = blocks * size // nn, blocks * size // nn // nx
    mid_n[...] = reduce(nn, n, narrow_peer, send_h, slots_n, sems_n)
    mid_h[...] = reduce(nx, x, x_peer, mid_n, slots_x, sems_hx)
    mine = full_h.at[pl.ds(pl.multiple_of(n * wide_piece + x * piece, piece), piece), :]
    mine[...] = reduce(nz, z, z_peer, mid_h, slots_z, sems_hz)
    exchange(nx, x, x_peer, lambda p: mine, mine, sems_hx2, first(full_h, nx, piece))
    block_n = chunk(full_h, n, wide_piece)
    exchange(nn, n, narrow_peer, lambda p: block_n, block_n, sems_n2, first(full_h, nn, wide_piece))
    out_h = pltpu.make_async_copy(full_h, hess_ref, sems_io.at[3])
    out_h.start()
    remainder = image
    for j in range(blocks):
        part = full_h[j * size : (j + 1) * size, :]
        remainder = remainder - mm(basis_ref[j], part, ((1,), (0,)))
    rest[...] = remainder
    out_rest = pltpu.make_async_copy(rest, rest_ref, sems_io.at[4])
    out_rest.start()
    send_g[...] = mm(remainder * scale, remainder, ((0,), (0,)))
    gstep = size // nn
    mid_g[...] = reduce(nn, n, narrow_peer, send_g, slots_gn, sems_gn)
    mid_g2[...] = reduce(nx, x, x_peer, mid_g, slots_gx, sems_x)
    own_g = chunk(full_g, n, gstep)
    own_g[...] = reduce(nz, z, z_peer, mid_g2, slots_gz, sems_z)
    exchange(nn, n, narrow_peer, lambda p: own_g, own_g, sems_gn2, first(full_g, nn, gstep))
    gram_ref[...] = full_g[...]
    out_h.wait()
    out_rest.wait()


def whole_step(panel, count, points, weight, basis, jacobi, agg, block, inverse, nn, nw, nz):
    blocks, rows, size = basis.shape
    f32, bf16 = jnp.float32, jnp.bfloat16
    pts = weight.shape[1]
    coarse = inverse.shape[1]
    vmem = pl.BlockSpec(memory_space=pltpu.VMEM)
    smem = pl.BlockSpec(memory_space=pltpu.SMEM)
    hbm = pl.BlockSpec(memory_space=pl.ANY)
    nx = nw // nz
    step, gstep = blocks * size // nn // nx, size // nn
    chunks, cols = nz + 2 * nx, nx * HALF
    dma = lambda *c: pltpu.SemaphoreType.DMA(c)
    lanes = max(nx // 2, 1)
    buf = pltpu.VMEM
    gather_sems = (dma(2), dma(3), dma(lanes, nz // 2), dma(nz // 2), dma(nz // 2 + 2))
    return pl.pallas_call(
        functools.partial(step_kernel, nn, nw, nz),
        name="step",
        out_shape=(
            jax.ShapeDtypeStruct((rows, size), f32),
            jax.ShapeDtypeStruct((blocks * size, size), f32),
            jax.ShapeDtypeStruct((size, size), f32),
        ),
        in_specs=[smem] * 2 + [vmem] * 2 + [hbm] + [vmem] * 2 + [hbm] * 2,
        out_specs=(hbm, hbm, vmem),
        scratch_shapes=[
            buf(basis.shape, f32),
            buf(block.shape, bf16),
            buf(inverse.shape, f32),
            buf((8, pts), f32),
            buf((nz, nx, 8, pts), f32),
            buf((nn, 8, pts), f32),
            buf((chunks, nx // 2, 8, pts), f32),
            buf((nn, 2, pts, pts), f32),
            buf((chunks, 3, nn * pts, cols), bf16),
            buf((nz, nx, coarse // 2, size), f32),
            buf((nx, nz, coarse // 2, size), f32),
            buf((nx, nz, coarse, size), f32),
            buf((nn, coarse, size), f32),
            buf((nn, coarse, size), f32),
            buf((nz, nx, HALF, 2 * size), bf16),
            buf((nx, nz, HALF, 2 * size), bf16),
            buf((pts + 2 * HALF, 2 * size), bf16),
            buf((2, HALF, 2 * size), bf16),
            buf((nn * pts, 2 * size), f32),
            buf((nn, pts, 2 * size), f32),
            buf((rows, size), f32),
            buf((blocks * size, size), f32),
            buf((nn, nx * step, size), f32),
            buf((nx * step, size), f32),
            buf((nx, step, size), f32),
            buf((step, size), f32),
            buf((nz, step, size), f32),
            buf((blocks * size, size), f32),
            buf((size, size), f32),
            buf((nn, gstep, size), f32),
            buf((gstep, size), f32),
            buf((nx, gstep, size), f32),
            buf((gstep, size), f32),
            buf((nz, gstep, size), f32),
            buf((size, size), f32),
            buf((rows, size), f32),
            pltpu.SemaphoreType.DMA((5,)),
            *([dma(2)] * 4), dma(2, 2),
            *gather_sems, *gather_sems,
            *([dma(2)] * 10),
        ],
        compiler_params=pltpu.CompilerParams(
            collective_id=0, has_side_effects=True, vmem_limit_bytes=60 * 1024 * 1024
        ),
    )(panel, count, points, weight, basis, jacobi, agg, block, inverse)


def finish_kernel(gram_ref, rest_hbm, hess_hbm, new_ref, hess_out, upper_ref, rest, hess, work, sems):
    size = gram_ref.shape[0]
    get_rest = pltpu.make_async_copy(rest_hbm, rest, sems.at[0])
    get_hess = pltpu.make_async_copy(hess_hbm, hess, sems.at[1])
    put_hess = pltpu.make_async_copy(hess, hess_out, sems.at[2])
    get_rest.start()
    get_hess.start()
    get_hess.wait()
    put_hess.start()
    factor(gram_ref[...], work)
    row = lax.broadcasted_iota(jnp.int32, (size, size), 0)
    col = lax.broadcasted_iota(jnp.int32, (size, size), 1)
    upper_ref[...] = jnp.where(row <= col, work[:, 0:size], 0.0)
    get_rest.wait()
    new_ref[...] = mm(rest[...], work[:, size:], ((1,), (1,)))
    put_hess.wait()


def finish(gram, rest, hess):
    f32 = jnp.float32
    size = gram.shape[0]
    vmem = pl.BlockSpec(memory_space=pltpu.VMEM)
    hbm = pl.BlockSpec(memory_space=pl.ANY)
    return pl.pallas_call(
        finish_kernel,
        name="finish",
        out_shape=(
            jax.ShapeDtypeStruct(rest.shape, f32),
            jax.ShapeDtypeStruct(hess.shape, f32),
            jax.ShapeDtypeStruct(gram.shape, f32),
        ),
        in_specs=[vmem, hbm, hbm],
        out_specs=(vmem, hbm, vmem),
        scratch_shapes=[
            pltpu.VMEM(rest.shape, f32),
            pltpu.VMEM(hess.shape, f32),
            pltpu.VMEM((size, 2 * size), f32),
            pltpu.SemaphoreType.DMA((3,)),
        ],
    )(gram, rest, hess)


def body(
    points, quad_weight, basis, jacobi, near_panel, near_count, near_block, agg_index, coarse_inverse, nz=NZ
):
    block_total, comps, point_count, rhs_count = basis.shape
    rest, hess, gram = whole_step(
        near_panel,
        near_count,
        points,
        quad_weight[None, :],
        basis.reshape(block_total, comps * point_count, rhs_count),
        jacobi,
        agg_index,
        near_block,
        coarse_inverse,
        lax.axis_size("narrow"),
        lax.axis_size("wide"),
        nz,
    )
    new_flat, hess, upper = finish(gram, rest, hess)
    return (
        new_flat.reshape(comps, point_count, rhs_count),
        hess.reshape(block_total, rhs_count, rhs_count),
        upper,
    )


def solution(mesh):
    in_specs = (
        P(None, ("narrow", "wide")),
        P(("narrow", "wide")),
        P(None, None, ("narrow", "wide"), None),
        P(None, ("narrow", "wide")),
        P(("narrow", "wide"), None),
        P(("narrow", "wide")),
        P(("narrow", "wide"), None, None, None),
        P(None, ("narrow", "wide")),
        P(None, "wide", "narrow"),
    )
    out_specs = (P(None, ("narrow", "wide"), None), P(), P())
    return jax.shard_map(body, mesh=mesh, in_specs=in_specs, out_specs=out_specs, check_vma=False)
```

```python
import functools

import jax
import jax.numpy as jnp
from jax import lax
from jax.experimental import pallas as pl
from jax.experimental.pallas import tpu as pltpu
from jax.sharding import PartitionSpec as P

NU = 0.3
DELTA2 = 1e-05
ELASTIC = 40.0
HIGH = lax.Precision.HIGHEST
MESH = pl.DeviceIdType.MESH
NZ = 8
PANEL = 32
GROUP = 16
HALF = 64


def mm(a, b, dims):
    return lax.dot_general(a, b, (dims, ((), ())), precision=HIGH, preferred_element_type=jnp.float32)


def drain(sem, ref):
    pltpu.make_async_copy(ref, ref, sem).wait()


def swap(count, me, device, src, dst, sems, whole, go):
    if not go:
        drain(sems.at[0], whole)
        drain(sems.at[1], whole)
        return

    def one(k, carry):
        peer = lax.rem(me + k, count)
        pltpu.make_async_remote_copy(
            src_ref=src(peer),
            dst_ref=dst,
            send_sem=sems.at[0],
            recv_sem=sems.at[1],
            device_id=device(peer),
            device_id_type=MESH,
        ).start()
        return carry

    lax.fori_loop(1, count, one, 0)


def exchange(count, me, device, src, dst, sems, whole):
    swap(count, me, device, src, dst, sems, whole, True)
    swap(count, me, device, src, dst, sems, whole, False)


def ring(count, me, device, block, half, send_sem, recv_sem, step):
    back = step - 1
    for way, peer, origin in ((0, me + 1, me + count - back), (1, me + count - 1, me + back)):
        peer, origin = lax.rem(peer, count), lax.rem(origin, count)
        ref = half(origin, way) if step == count // 2 else block(origin)
        pltpu.make_async_remote_copy(
            src_ref=ref,
            dst_ref=ref,
            send_sem=send_sem,
            recv_sem=recv_sem,
            device_id=device(peer),
            device_id_type=MESH,
        ).start()


def slots_sum(ref, count):
    total = ref[0]
    for k in range(1, count):
        total = total + ref[k]
    return total


def greet(groups, others):
    barrier = pltpu.get_barrier_semaphore()
    for count, me, device in groups:

        def one(k, carry):
            pl.semaphore_signal(barrier, inc=1, device_id=device(lax.rem(me + k, count)), device_id_type=MESH)
            return carry

        lax.fori_loop(1, count, one, 0)
    for peer in others:
        pl.semaphore_signal(barrier, inc=1, device_id=peer, device_id_type=MESH)
    return barrier, sum(count - 1 for count, _, _ in groups) + len(others)


def factor(gram, work):
    size = gram.shape[0]
    rows = lax.broadcasted_iota(jnp.int32, (size, size), 0)
    cols = lax.broadcasted_iota(jnp.int32, (size, size), 1)
    work[:, 0:size] = gram
    work[:, size:] = (rows == cols).astype(jnp.float32)
    sub = lax.broadcasted_iota(jnp.int32, (PANEL, size), 0)
    for base in range(0, size, PANEL):
        sides = [work[base : base + PANEL, 0:size], work[base : base + PANEL, size:]]
        for k in range(0, PANEL, GROUP):
            lefts = [
                jnp.broadcast_to(sides[0][:, base + k + j : base + k + j + 1], (PANEL, size)) for j in range(GROUP)
            ]
            tops = [[side[k + j : k + j + 1, :] for side in sides] for j in range(GROUP)]
            for j in range(GROUP):
                inv = lax.rsqrt(lefts[j][k + j : k + j + 1, :])
                lefts[j] = lefts[j] * inv
                tops[j] = [top * inv for top in tops[j]]
                for i in range(j + 1, GROUP):
                    share = lefts[j][k + i : k + i + 1, :]
                    lefts[i] = lefts[i] - lefts[j] * share
                    tops[i] = [top - share * done for top, done in zip(tops[i], tops[j])]
            for s in range(2):
                new = sides[s]
                for j in range(GROUP):
                    new = new - lefts[j] * tops[j][s]
                new = jnp.where(sub >= k + GROUP, new, sides[s])
                for j in range(GROUP):
                    new = jnp.where(sub == k + j, tops[j][s], new)
                sides[s] = new
        work[base : base + PANEL, 0:size] = sides[0]
        work[base : base + PANEL, size:] = sides[1]
        if base + PANEL < size:
            panel = jnp.concatenate(sides, axis=1)
            below = mm(sides[0], panel, ((0,), (0,)))
            work[base + PANEL :, :] = work[base + PANEL :, :] - below[base + PANEL :, :]


def column(row, points):
    return jnp.transpose(jnp.broadcast_to(row, (points, points)))


def step_kernel(
    nn, nw, nz,
    panel_ref, count_ref, points_ref, weight_ref, basis_hbm, jacobi_ref, agg_ref, block_hbm, inverse_hbm,
    rest_ref, hess_ref, gram_ref,
    basis_ref, block_ref, inverse_ref,
    info, info_w, info_n, sources, columns, green,
    rhs_a, rhs_b, rhs_all, parts, part_slots, fields_a, fields_b, window, halo, far, far_slots, near,
    send_h, slots_n, mid_n, slots_x, mid_h, slots_z, full_h,
    send_g, slots_gn, mid_g, slots_gx, mid_g2, slots_gz, full_g,
    rest,
    sems_io, sems_ix, sems_iz, sems_in, sems_cn, sems_halo,
    sems_cax, sems_cs, sems_caz, sems_cbz, sems_cbx,
    sems_ax, sems_as, sems_az, sems_bz, sems_bx, sems_far,
    sems_n, sems_hx, sems_hz, sems_hx2, sems_n2, sems_gn, sems_x, sems_z, sems_gn2,
):
    f32, bf16 = jnp.float32, jnp.bfloat16
    n = lax.axis_index("narrow")
    w = lax.axis_index("wide")
    x, z = w // nz, lax.rem(w, nz)
    nx = nw // nz
    blocks, size = basis_ref.shape[0], basis_ref.shape[2]
    points = weight_ref.shape[1]
    coarse = inverse_ref.shape[1]
    flat = n * nw + w
    total = nn * nw

    def flat_peer(p):
        return {"narrow": p // nw, "wide": lax.rem(p, nw)}

    before, after = flat_peer(lax.rem(flat + total - 1, total)), flat_peer(lax.rem(flat + 1, total))
    def narrow_peer(p):
        return {"narrow": p}

    def z_peer(p):
        return {"wide": x * nz + p}

    def x_peer(p):
        return {"wide": p * nz + z}

    barrier, greeted = greet(((nn, n, narrow_peer), (nx, x, x_peer), (nz, z, z_peer)), (before, after))
    loads = [
        pltpu.make_async_copy(src, dst, sems_io.at[i])
        for i, (src, dst) in enumerate(((basis_hbm, basis_ref), (inverse_hbm, inverse_ref), (block_hbm, block_ref)))
    ]
    for load in loads:
        load.start()

    lanes = max(nx // 2, 1)

    def gathering(buf_a, buf_b, cut, sem_ax, sem_send, sem_az, sem_bz, sem_bx):
        deep, cross = nz // 2, nx // 2

        def a_first(go):
            swap(nx, x, x_peer, lambda p: buf_a.at[z, x], buf_a.at[z, x], sem_ax, buf_a.at[0, 0 : nx - 1], go)

        def a_ring(j, step, go):
            if not go:
                drain(sem_az.at[j, step - 1], buf_a.at[0:2, 0:2] if step < deep else buf_a.at[0, 0:2])
                return
            ring(
                nz, z, z_peer,
                lambda p: buf_a.at[p, 2 * j : 2 * j + 2],
                lambda p, way: buf_a.at[p, 2 * j + way],
                sem_send.at[0], sem_az.at[j, step - 1], step,
            )

        def part(ref, way):
            return ref.at[:cut] if way == 0 else ref.at[cut:]

        def b_ring(step, go):
            if not go:
                drain(sem_bz.at[step - 1], buf_b.at[0, 0:2] if step < deep else buf_b.at[0, 0])
                return
            ring(
                nz, z, z_peer,
                lambda p: buf_b.at[x, p],
                lambda p, way: part(buf_b.at[x, p], way),
                sem_send.at[1], sem_bz.at[step - 1], step,
            )

        def bx_ring(shift, step, go):
            signs = [sign for at, sign in ((2 * shift - 1, -1), (2 * shift, 1)) if 0 <= at < nz]
            if not go:
                drain(sem_bx.at[shift], buf_b.at[0, 0 : len(signs) * (2 if step < cross else 1)])
                return
            for sign in signs:
                q = lax.rem(z + nz + sign * shift, nz)
                ring(
                    nx, x, x_peer,
                    lambda p: buf_b.at[p, q],
                    lambda p, way: part(buf_b.at[p, q], way),
                    sem_send.at[2], sem_bx.at[shift if step == 1 else deep + 1], step,
                )

        def close():
            if cross > 1:
                drain(sem_bx.at[deep + 1], buf_b.at[0])
            drain(sem_send.at[0], buf_a.at[0 : nz - 1])
            drain(sem_send.at[1], buf_b.at[0, 0 : nz - 1])
            drain(sem_send.at[2], buf_b.at[0 : nx - 1])

        return a_first, a_ring, b_ring, bx_ring, close

    def run_gather(steps, opened, own, arrived, crossed):
        a_first, a_ring, b_ring, bx_ring, close = steps
        deep, wide_steps = nz // 2, nx // 2

        def next_b(step):
            b_ring(step, False)
            if step < deep:
                b_ring(step + 1, True)
            bx_ring(step, 1, True)

        def next_x(shift):
            bx_ring(shift, 1, False)
            if wide_steps > 1:
                bx_ring(shift, 2, True)

        a_first(True)
        b_ring(1, True)
        bx_ring(0, 1, True)
        opened()
        a_first(False)
        for j in range(lanes):
            a_ring(j, 1, True)
        next_b(1)
        next_x(0)
        own()
        if deep > 1:
            next_b(2)
        for step in range(1, deep + 1):
            for j in range(lanes):
                a_ring(j, step, False)
                if step < deep:
                    a_ring(j, step + 1, True)
            if step + 2 <= deep:
                next_b(step + 2)
            if step < deep:
                next_x(step)
            if step == deep - 1:
                next_x(deep)
            arrived(step)
            if step == max(1, deep - 2):
                crossed(0)
            if step == deep - 1:
                crossed(1)
        close()
        if wide_steps > 1:
            crossed(2)

    info[...] = jnp.zeros_like(info)
    info[0:2, :] = points_ref[...]
    info[2:3, :] = ELASTIC * weight_ref[...]
    info_n[n] = info[...]
    info_w[z, x] = info[...]

    ids = lax.broadcasted_iota(jnp.int32, (coarse, points), 0)
    member = [(ids == agg_ref[a : a + 1, :]).astype(f32) for a in range(2)]
    loads[0].wait()
    newest = [basis_ref[blocks - 1, a * points : (a + 1) * points, :] for a in range(2)]
    rhs = mm(member[0], newest[0], ((1,), (0,))) + mm(member[1], newest[1], ((1,), (0,)))
    rhs_a[z, x] = rhs[0 : coarse // 2, :]
    rhs_b[x, z] = rhs[coarse // 2 :, :]
    pl.semaphore_wait(barrier, greeted)
    swap(nx, x, x_peer, lambda p: info, info_w.at[z, x], sems_ix, info_w.at[0, 0 : nx - 1], True)
    swap(nn, n, narrow_peer, lambda p: info, info_n.at[n], sems_in, info_n.at[0 : nn - 1], True)
    chunks = nz + 2 * nx
    tall = 32
    pairs = nx // 2

    def spread_info():
        swap(nx, x, x_peer, lambda p: info, info_w.at[z, x], sems_ix, info_w.at[0, 0 : nx - 1], False)
        swap(nz, z, z_peer, lambda p: info_w.at[z], info_w.at[z], sems_iz, info_w.at[0 : nz - 1], True)

    def prepare():
        swap(nn, n, narrow_peer, lambda p: info, info_n.at[n], sems_in, info_n.at[0 : nn - 1], False)
        swap(nz, z, z_peer, lambda p: info_w.at[z], info_w.at[z], sems_iz, info_w.at[0 : nz - 1], False)
        lane = lax.broadcasted_iota(jnp.int32, (8, points), 1)
        for p in range(nz):
            for m in range(pairs):
                one, two = info_w[p, 2 * m], info_w[p, 2 * m + 1]
                sources[p, m] = jnp.where(lane < HALF, one, pltpu.roll(two, HALF, 1))
        for p in range(nx):
            for h in range(2):
                for m in range(pairs):
                    at = h * (nz // 2) + 2 * m
                    one, two = info_w[at, p], info_w[at + 1, p]
                    sources[nz + 2 * p + h, m] = jnp.where(lane < HALF, pltpu.roll(one, HALF, 1), two)
        for t in range(nn):
            tile = info_n[t]
            for a in range(2):
                columns[t, a] = column(tile[a : a + 1, :], points)

    def evaluate(first, last):
        def unit(i, carry):
            c, t = i // nn, lax.rem(i, nn)
            for m in range(pairs):
                src = sources[c, m]
                sx, sy, sw = src[0:1, :], src[1:2, :], src[2:3, :]
                for r in range(0, points, tall):
                    dx = columns[t, 0, r : r + tall, :] - sx
                    dy = columns[t, 1, r : r + tall, :] - sy
                    xx, yy = dx * dx, dy * dy
                    square = xx + yy + DELTA2
                    inv = 1.0 / square
                    log_part = (-0.5 * (3.0 - 4.0 * NU)) * jnp.log(square)
                    rows = pl.ds(pl.multiple_of(t * points + r, tall), tall)
                    cols = slice(m * points, (m + 1) * points)
                    green[c, 0, rows, cols] = (sw * (log_part + xx * inv)).astype(bf16)
                    green[c, 1, rows, cols] = (sw * (dx * dy * inv)).astype(bf16)
                    green[c, 2, rows, cols] = (sw * (log_part + yy * inv)).astype(bf16)
            return carry

        lax.fori_loop(first, last, unit, 0)

    done = [0]

    def fill(share):
        last = min(done[0] + share * chunks * nn // 128, chunks * nn)
        evaluate(done[0], last)
        done[0] = last

    def rhs_arrived(step):
        if step == 1:
            prepare()
        fill(20)

    run_gather(
        gathering(rhs_a, rhs_b, 16, sems_cax, sems_cs, sems_caz, sems_cbz, sems_cbx),
        spread_info, lambda: None, rhs_arrived, lambda step: None,
    )
    for p in range(nx):
        for q in range(nz):
            rhs_all[p, q, 0 : coarse // 2, :] = rhs_a[q, p]
            rhs_all[p, q, coarse // 2 :, :] = rhs_b[p, q]
    loads[1].wait()

    inverse = inverse_ref[...].reshape(nn * coarse, nw * coarse)
    parts[...] = mm(inverse, rhs_all[...].reshape(nw * coarse, size), ((1,), (0,))).reshape(nn, coarse, size)
    swap(nn, n, narrow_peer, lambda p: parts.at[p], part_slots.at[n], sems_cn, part_slots.at[0 : nn - 1], True)
    part_slots[n] = parts[n]
    fill(36)
    swap(nn, n, narrow_peer, lambda p: parts.at[p], part_slots.at[n], sems_cn, part_slots.at[0 : nn - 1], False)
    sol = slots_sum(part_slots, nn)
    for a in range(2):
        lifted = mm(member[a], sol, ((0,), (0,)))
        field = (column(jacobi_ref[a : a + 1, :], points) * newest[a] + lifted).astype(bf16)
        window[HALF : HALF + points, a * size : (a + 1) * size] = field
    fields_a[z, x] = window[HALF : 2 * HALF, :]
    fields_b[x, z] = window[2 * HALF : 3 * HALF, :]

    def halo_copy(way, src, peer, go):
        copy = pltpu.make_async_remote_copy(
            src_ref=src, dst_ref=halo.at[way], send_sem=sems_halo.at[0, way], recv_sem=sems_halo.at[1, way],
            device_id=peer, device_id_type=MESH,
        )
        if go:
            copy.start()
        else:
            copy.wait()

    def halos(go):
        halo_copy(0, fields_b.at[x, z], after, go)
        halo_copy(1, fields_a.at[z, x], before, go)

    def accumulate_rows(c, field, first, i):
        left, right = field[:, 0:size], field[:, size:]
        rows = pl.ds(pl.multiple_of(i * 2 * points, 2 * points), 2 * points)
        cross = jnp.dot(green[c, 1, rows, :], field, preferred_element_type=f32)
        one = jnp.dot(green[c, 0, rows, :], left, preferred_element_type=f32) + cross[:, size:]
        two = jnp.dot(green[c, 2, rows, :], right, preferred_element_type=f32) + cross[:, 0:size]
        if first:
            far[rows, 0:size] = one
            far[rows, size:] = two
        else:
            far[rows, 0:size] = far[rows, 0:size] + one
            far[rows, size:] = far[rows, size:] + two

    def accumulate(c, field, first):
        def rows_of(i, carry):
            accumulate_rows(c, field, first, i)
            return carry

        lax.fori_loop(0, nn // 2, rows_of, 0)

    def send_far(p):
        pltpu.make_async_remote_copy(
            src_ref=far.at[pl.ds(pl.multiple_of(p * points, points), points), :],
            dst_ref=far_slots.at[n],
            send_sem=sems_far.at[0],
            recv_sem=sems_far.at[1],
            device_id=narrow_peer(p),
            device_id_type=MESH,
        ).start()

    def part_b(p, h):
        return fields_b[p, h * (nz // 2) : (h + 1) * (nz // 2)].reshape(nz // 2 * HALF, 2 * size)

    def finish_far(p):
        p = lax.rem(p, nx)
        pairs_of = nn // 2
        for shift in sorted(range(pairs_of), key=lambda k: -min(k, pairs_of - k)):
            i = lax.rem(n // 2 + shift, pairs_of)
            for h in range(2):
                accumulate_rows(nz + 2 * p + h, part_b(p, h), False, i)
            if shift:
                send_far(2 * i)
                send_far(2 * i + 1)
            else:
                send_far(2 * i + 1 - lax.rem(n, 2))

    def take_a(p, first=False):
        p = lax.rem(p, nz)
        accumulate(p, fields_a[p].reshape(nx * HALF, 2 * size), first)

    def take_b(p):
        p = lax.rem(p, nx)
        for h in range(2):
            part = fields_b[p, h * (nz // 2) : (h + 1) * (nz // 2)]
            accumulate(nz + 2 * p + h, part.reshape(nz // 2 * HALF, 2 * size), False)

    def near_field():
        halos(False)
        loads[2].wait()
        window[0:HALF, :] = halo[0]
        window[HALF + points :, :] = halo[1]
        q = block_ref.shape[2] // 2
        panels, slots = block_ref.shape[0], block_ref.shape[1]

        reach = points + 2 * HALF
        row_id = lax.broadcasted_iota(jnp.int32, (q, reach), 0)
        col_id = lax.broadcasted_iota(jnp.int32, (q, reach), 1)

        def one_panel(p, carry):
            live = jnp.full((q, reach), count_ref[p], jnp.int32)
            picks = []
            for k in range(slots):
                start = jnp.full((q, reach), (panel_ref[p, k] - flat * panels) * q + HALF, jnp.int32)
                picks.append(((col_id == start + row_id) & (live > k)).astype(f32))
            pick = jnp.concatenate(picks, axis=0).astype(bf16)
            rows = jnp.dot(pick, window[...], preferred_element_type=f32).astype(bf16)
            total = jnp.zeros((2 * q, size), f32)
            for k in range(slots):
                one = rows[k * q : (k + 1) * q, :]
                both = jnp.concatenate([one[:, 0:size], one[:, size:]], axis=0)
                total = total + jnp.dot(block_ref[p, k], both, preferred_element_type=f32)
            for a in range(2):
                near[pl.ds(pl.multiple_of(a * points + p * q, q), q), :] = total[a * q : (a + 1) * q, :]
            return carry

        lax.fori_loop(0, panels, one_panel, 0)

    def opened():
        halos(True)
        fill(12)

    def arrived(step):
        fill(128)
        take_a(z + nz - step)
        if step < nz // 2:
            take_a(z + step)
        if step == 1:
            near_field()

    def crossed(step):
        if step == 0:
            take_b(x)
            return
        if step == 2:
            finish_far(x + nx - step)
            return
        take_b(x + nx - step)
        if step < nx // 2:
            take_b(x + step)

    run_gather(
        gathering(fields_a, fields_b, HALF // 2, sems_ax, sems_as, sems_az, sems_bz, sems_bx),
        opened, lambda: take_a(z, True), arrived, crossed,
    )

    if nx == 2:
        for shift in range(1, nn):
            send_far(lax.rem(n + shift, nn))
    far_slots[n] = far[pl.ds(pl.multiple_of(n * points, points), points), :]
    base = jnp.concatenate([near[0:points, :], near[points:, :]], axis=1)
    base = base + 0.5 * window[HALF : HALF + points, :].astype(f32)
    drain(sems_far.at[0], far_slots.at[0 : nn - 1])
    drain(sems_far.at[1], far_slots.at[0 : nn - 1])
    base = base + slots_sum(far_slots, nn)
    image = jnp.concatenate([base[:, 0:size], base[:, size:]], axis=0)

    spread = column(weight_ref[...], points)
    scale = jnp.concatenate([spread, spread], axis=0)
    weighted = image * scale
    for j in range(blocks):
        send_h[j * size : (j + 1) * size, :] = mm(basis_ref[j], weighted, ((0,), (0,)))
    def chunk(ref, p, rows):
        return ref.at[pl.ds(pl.multiple_of(p * rows, rows), rows), :]

    def first(ref, count, rows):
        return ref.at[0 : (count - 1) * rows, :]

    def reduce(count, me, device, src, slots, sems):
        piece = slots.shape[1]
        whole = slots.at[0 : count - 1]
        pick = (lambda p: chunk(src, p, piece)) if src.shape[0] > piece else (lambda p: src)
        swap(count, me, device, pick, slots.at[me], sems, whole, True)
        slots[me] = pick(me)[...]
        swap(count, me, device, pick, slots.at[me], sems, whole, False)
        return slots_sum(slots, count)

    wide_piece, piece = blocks * size // nn, blocks * size // nn // nx
    mid_n[...] = reduce(nn, n, narrow_peer, send_h, slots_n, sems_n)
    mid_h[...] = reduce(nx, x, x_peer, mid_n, slots_x, sems_hx)
    mine = full_h.at[pl.ds(pl.multiple_of(n * wide_piece + x * piece, piece), piece), :]
    mine[...] = reduce(nz, z, z_peer, mid_h, slots_z, sems_hz)
    exchange(nx, x, x_peer, lambda p: mine, mine, sems_hx2, first(full_h, nx, piece))
    block_n = chunk(full_h, n, wide_piece)
    exchange(nn, n, narrow_peer, lambda p: block_n, block_n, sems_n2, first(full_h, nn, wide_piece))
    out_h = pltpu.make_async_copy(full_h, hess_ref, sems_io.at[3])
    out_h.start()
    remainder = image
    for j in range(blocks):
        part = full_h[j * size : (j + 1) * size, :]
        remainder = remainder - mm(basis_ref[j], part, ((1,), (0,)))
    rest[...] = remainder
    out_rest = pltpu.make_async_copy(rest, rest_ref, sems_io.at[4])
    out_rest.start()
    send_g[...] = mm(remainder * scale, remainder, ((0,), (0,)))
    gstep = size // nn
    mid_g[...] = reduce(nn, n, narrow_peer, send_g, slots_gn, sems_gn)
    mid_g2[...] = reduce(nx, x, x_peer, mid_g, slots_gx, sems_x)
    own_g = chunk(full_g, n, gstep)
    own_g[...] = reduce(nz, z, z_peer, mid_g2, slots_gz, sems_z)
    exchange(nn, n, narrow_peer, lambda p: own_g, own_g, sems_gn2, first(full_g, nn, gstep))
    gram_ref[...] = full_g[...]
    out_h.wait()
    out_rest.wait()


def whole_step(panel, count, points, weight, basis, jacobi, agg, block, inverse, nn, nw, nz):
    blocks, rows, size = basis.shape
    f32, bf16 = jnp.float32, jnp.bfloat16
    pts = weight.shape[1]
    coarse = inverse.shape[1]
    vmem = pl.BlockSpec(memory_space=pltpu.VMEM)
    smem = pl.BlockSpec(memory_space=pltpu.SMEM)
    hbm = pl.BlockSpec(memory_space=pl.ANY)
    nx = nw // nz
    step, gstep = blocks * size // nn // nx, size // nn
    chunks, cols = nz + 2 * nx, nx * HALF
    dma = lambda *c: pltpu.SemaphoreType.DMA(c)
    lanes = max(nx // 2, 1)
    buf = pltpu.VMEM
    gather_sems = (dma(2), dma(3), dma(lanes, nz // 2), dma(nz // 2), dma(nz // 2 + 2))
    return pl.pallas_call(
        functools.partial(step_kernel, nn, nw, nz),
        name="step",
        out_shape=(
            jax.ShapeDtypeStruct((rows, size), f32),
            jax.ShapeDtypeStruct((blocks * size, size), f32),
            jax.ShapeDtypeStruct((size, size), f32),
        ),
        in_specs=[smem] * 2 + [vmem] * 2 + [hbm] + [vmem] * 2 + [hbm] * 2,
        out_specs=(hbm, hbm, vmem),
        scratch_shapes=[
            buf(basis.shape, f32),
            buf(block.shape, bf16),
            buf(inverse.shape, f32),
            buf((8, pts), f32),
            buf((nz, nx, 8, pts), f32),
            buf((nn, 8, pts), f32),
            buf((chunks, nx // 2, 8, pts), f32),
            buf((nn, 2, pts, pts), f32),
            buf((chunks, 3, nn * pts, cols), bf16),
            buf((nz, nx, coarse // 2, size), f32),
            buf((nx, nz, coarse // 2, size), f32),
            buf((nx, nz, coarse, size), f32),
            buf((nn, coarse, size), f32),
            buf((nn, coarse, size), f32),
            buf((nz, nx, HALF, 2 * size), bf16),
            buf((nx, nz, HALF, 2 * size), bf16),
            buf((pts + 2 * HALF, 2 * size), bf16),
            buf((2, HALF, 2 * size), bf16),
            buf((nn * pts, 2 * size), f32),
            buf((nn, pts, 2 * size), f32),
            buf((rows, size), f32),
            buf((blocks * size, size), f32),
            buf((nn, nx * step, size), f32),
            buf((nx * step, size), f32),
            buf((nx, step, size), f32),
            buf((step, size), f32),
            buf((nz, step, size), f32),
            buf((blocks * size, size), f32),
            buf((size, size), f32),
            buf((nn, gstep, size), f32),
            buf((gstep, size), f32),
            buf((nx, gstep, size), f32),
            buf((gstep, size), f32),
            buf((nz, gstep, size), f32),
            buf((size, size), f32),
            buf((rows, size), f32),
            pltpu.SemaphoreType.DMA((5,)),
            *([dma(2)] * 4), dma(2, 2),
            *gather_sems, *gather_sems,
            *([dma(2)] * 10),
        ],
        compiler_params=pltpu.CompilerParams(
            collective_id=0, has_side_effects=True, vmem_limit_bytes=60 * 1024 * 1024
        ),
    )(panel, count, points, weight, basis, jacobi, agg, block, inverse)


def finish_kernel(gram_ref, rest_hbm, hess_hbm, new_ref, hess_out, upper_ref, rest, hess, work, sems):
    size = gram_ref.shape[0]
    get_rest = pltpu.make_async_copy(rest_hbm, rest, sems.at[0])
    get_hess = pltpu.make_async_copy(hess_hbm, hess, sems.at[1])
    put_hess = pltpu.make_async_copy(hess, hess_out, sems.at[2])
    get_rest.start()
    get_hess.start()
    get_hess.wait()
    put_hess.start()
    factor(gram_ref[...], work)
    row = lax.broadcasted_iota(jnp.int32, (size, size), 0)
    col = lax.broadcasted_iota(jnp.int32, (size, size), 1)
    upper_ref[...] = jnp.where(row <= col, work[:, 0:size], 0.0)
    get_rest.wait()
    new_ref[...] = mm(rest[...], work[:, size:], ((1,), (1,)))
    put_hess.wait()


def finish(gram, rest, hess):
    f32 = jnp.float32
    size = gram.shape[0]
    vmem = pl.BlockSpec(memory_space=pltpu.VMEM)
    hbm = pl.BlockSpec(memory_space=pl.ANY)
    return pl.pallas_call(
        finish_kernel,
        name="finish",
        out_shape=(
            jax.ShapeDtypeStruct(rest.shape, f32),
            jax.ShapeDtypeStruct(hess.shape, f32),
            jax.ShapeDtypeStruct(gram.shape, f32),
        ),
        in_specs=[vmem, hbm, hbm],
        out_specs=(vmem, hbm, vmem),
        scratch_shapes=[
            pltpu.VMEM(rest.shape, f32),
            pltpu.VMEM(hess.shape, f32),
            pltpu.VMEM((size, 2 * size), f32),
            pltpu.SemaphoreType.DMA((3,)),
        ],
    )(gram, rest, hess)


def body(
    points, quad_weight, basis, jacobi, near_panel, near_count, near_block, agg_index, coarse_inverse, nz=NZ
):
    block_total, comps, point_count, rhs_count = basis.shape
    rest, hess, gram = whole_step(
        near_panel,
        near_count,
        points,
        quad_weight[None, :],
        basis.reshape(block_total, comps * point_count, rhs_count),
        jacobi,
        agg_index,
        near_block,
        coarse_inverse,
        lax.axis_size("narrow"),
        lax.axis_size("wide"),
        nz,
    )
    new_flat, hess, upper = finish(gram, rest, hess)
    return (
        new_flat.reshape(comps, point_count, rhs_count),
        hess.reshape(block_total, rhs_count, rhs_count),
        upper,
    )


def solution(mesh):
    in_specs = (
        P(None, ("narrow", "wide")),
        P(("narrow", "wide")),
        P(None, None, ("narrow", "wide"), None),
        P(None, ("narrow", "wide")),
        P(("narrow", "wide"), None),
        P(("narrow", "wide")),
        P(("narrow", "wide"), None, None, None),
        P(None, ("narrow", "wide")),
        P(None, "wide", "narrow"),
    )
    out_specs = (P(None, ("narrow", "wide"), None), P(), P())
    return jax.shard_map(body, mesh=mesh, in_specs=in_specs, out_specs=out_specs, check_vma=False)
```
